32 devices in a mesh: rows: 4 (over y, core), feat: 8 (over z, x).
Axes of the slice: x: 2, y: 2, z: 4, core: 2. Of those that a mesh axis runs over, the one named last changes fastest.
Arguments:
- margins: float32 [12288, 32], P(('rows', 'feat')), may hold values from -30 to 260
- labels: int32 [12288], P(('rows', 'feat')), may hold values from 0 to 31
- row_bins: int32 [1024, 12288], P('feat', 'rows'), may hold values from 0 to 63
- parents: int32 [12288], P('rows'), may hold values from 0 to 7
- split_feature: int32 [8], replicated, may hold values from 0 to 1023
- split_bin: int32 [8], replicated, may hold values from 16 to 47
- leaf_values: float32 [16, 32], replicated, may hold values from -4 to 4
Outputs:
- split_gains: float32 [16, 1024, 64], P('rows', 'feat')
- node_totals: float32 [16, 64], replicated
The draws below stay inside these ranges and needn't reach their ends.
All inputs are finite; a program needn't handle non-finite values.
Results may differ from the reference program's by a relative error of at most 0.0017.
Values may be sent and summed in bfloat16 or wider, within the bound.
No kernel may reach another device: no remote copies, remote signals or barrier semaphores. Data moves between devices by JAX's collectives and lax.ppermute only.
A program may use at most 192 MiB of HBM per device.

```python
import math
import jax
import jax.numpy as jnp
import numpy as np
from jax import lax

C = 32
F = 1024
BINS = 64
NODES = 16
PARENTS = 8
TOTAL_ROWS = 12288


def draw_margins(key, part):
    first_key = jax.random.fold_in(key, 0)
    base = jnp.clip(jax.random.normal(first_key, (TOTAL_ROWS, C), jnp.float32), -8.0, 8.0)
    row_ids = jnp.arange(TOTAL_ROWS, dtype=jnp.int32)
    column_ids = jnp.arange(C, dtype=jnp.int32)
    position = row_ids.astype(jnp.float32) / TOTAL_ROWS
    base = base + jnp.where(column_ids[None, :] == 0, 3.0 * position[:, None], 0.0)
    return base


def with_ends(result, key, least, largest):
    place = [jax.random.randint(jax.random.fold_in(key, axis), (), 0, length) for axis, length in enumerate(result.shape)]
    main_axis = result.shape.index(max(result.shape))
    beside = place[:main_axis] + [(place[main_axis] + 1) % result.shape[main_axis]] + place[main_axis + 1:]
    return result.at[tuple(place)].set(least).at[tuple(beside)].set(largest)


def rank_table(count, lean):
    loads = [(1 << 20) // math.isqrt(rank ** lean) + 1 for rank in range(1, count + 1)]
    deviation = 1 + sum(loads) // (1 << 30)
    return np.cumsum(np.array([max(1, weight // deviation) for weight in loads]))


def ranked_ids(key, shape, amount, slope):
    grid = rank_table(amount, slope)
    pick = jax.random.randint(jax.random.fold_in(key, 1), shape, 0, int(grid[amount - 1]))
    rank = jnp.searchsorted(jnp.asarray(grid, jnp.int32), pick, side="right")
    return jax.random.permutation(jax.random.fold_in(key, 2), amount)[rank].astype(jnp.int32)


def normal_values(own_key, dims, scale, reach, held_as=jnp.bfloat16):
    result = jax.random.normal(own_key, dims, jnp.float32) * scale
    return jnp.minimum(jnp.maximum(result, -reach), reach).astype(held_as)


def setup_inputs(seed: int = 0) -> dict:
    arg_keys = jax.random.split(jax.random.key(seed), 8)
    return {
        "margins": draw_margins(jax.random.fold_in(arg_keys[7], 71), 0),
        "labels": with_ends(jax.random.randint(arg_keys[1], (TOTAL_ROWS,), 0, C), jax.random.fold_in(arg_keys[1], 1), 0, C - 1).astype(jnp.int32),
        "row_bins": with_ends(jax.random.randint(arg_keys[2], (F, TOTAL_ROWS), 0, BINS), jax.random.fold_in(arg_keys[2], 1), 0, BINS - 1).astype(jnp.int32),
        "parents": with_ends(ranked_ids(arg_keys[3], (TOTAL_ROWS,), PARENTS, 2), jax.random.fold_in(arg_keys[3], 3), 0, PARENTS - 1).astype(jnp.int32),
        "split_feature": with_ends(jax.random.randint(arg_keys[4], (PARENTS,), 0, F), jax.random.fold_in(arg_keys[4], 1), 0, F - 1).astype(jnp.int32),
        "split_bin": with_ends(jax.random.randint(arg_keys[5], (PARENTS,), BINS // 4, 3 * BINS // 4), jax.random.fold_in(arg_keys[5], 1), BINS // 4, (3 * BINS // 4) - 1).astype(jnp.int32),
        "leaf_values": normal_values(arg_keys[6], (NODES, C), 1.0, 4.0, jnp.float32),
    }


hess_ridge = 1.0


def gain_scores(left_sums, totals, classes):
    grad_left = left_sums[..., :classes]
    hess_left = left_sums[..., classes:]
    grad_whole = totals[..., :classes]
    hess_whole = totals[..., classes:]
    grad_right = grad_whole - grad_left
    hess_right = hess_whole - hess_left
    score = grad_left * grad_left / (hess_left + hess_ridge) + grad_right * grad_right / (hess_right + hess_ridge) - grad_whole * grad_whole / (hess_whole + hess_ridge)
    return jnp.mean(score, axis=-1)


def reference(margins, labels, row_bins, parents, split_feature, split_bin, leaf_values):
    chosen = jnp.take_along_axis(row_bins, split_feature[parents][None, :], axis=0)[0]
    node_ids = 2 * parents + (chosen > split_bin[parents]).astype(jnp.int32)
    logits = margins + leaf_values[node_ids]
    probabilities = jax.nn.softmax(logits, axis=1)
    label_hot = (labels[:, None] == jnp.arange(C, dtype=jnp.int32)[None, :]).astype(jnp.float32)
    gradient = probabilities - label_hot
    hessian = 2.0 * probabilities * (1.0 - probabilities)
    grad_hess = jnp.concatenate([gradient, hessian], axis=1).astype(jnp.bfloat16).astype(jnp.float32)
    node_totals = jax.ops.segment_sum(grad_hess, node_ids, num_segments=NODES)

    def feature_hist(column):
        keys = node_ids * BINS + column
        summed = jax.ops.segment_sum(grad_hess, keys, num_segments=NODES * BINS)
        return summed.reshape(NODES, BINS, 2 * C)

    histogram = lax.map(feature_hist, row_bins)
    left_sums = jnp.cumsum(histogram, axis=2)
    scores = gain_scores(left_sums, node_totals[None, :, None, :], C)
    return jnp.transpose(scores, (1, 0, 2)), node_totals
```

```python
import functools

import jax
import jax.numpy as jnp
from jax import lax
from jax.experimental import pallas as pl
from jax.experimental.pallas import tpu as pltpu
from jax.sharding import PartitionSpec as P

BINS = 64
LANES = 128
TILE = 16
GROUP_NODES = 4
CHUNK = 512
COPY_TILES = 4
COLS = 256

hess_ridge = 1.0

F32 = jnp.float32
BF16 = jnp.bfloat16
I32 = jnp.int32
NT = (((1,), (1,)), ((), ()))
VMEM = pl.BlockSpec(memory_space=pltpu.VMEM)
SMEM = pl.BlockSpec(memory_space=pltpu.SMEM)


def cdiv(a, b):
    return -(-a // b)


def iota(shape, dim):
    return lax.broadcasted_iota(I32, shape, dim)


def first_message_kernel(parent_count, nf, scal, margins, labels, bins, parents, out):
    own, classes = margins.shape
    feat_dev = bins.shape[0]
    out[0:classes, :] = margins[...].T
    par = parents[...]
    right = jnp.zeros(par.shape, F32)
    for p in range(parent_count):
        local = scal[p] - scal[2 * parent_count]
        owned = jnp.logical_and(local >= 0, local < feat_dev)
        threshold = jnp.where(owned, scal[parent_count + p], BINS)
        row = bins[pl.ds(jnp.clip(local, 0, feat_dev - 1), 1), :]
        right = right + jnp.where((par == p) & (row > threshold), 1.0, 0.0)
    out[classes : classes + 8, :] = jnp.broadcast_to(labels[...].astype(F32), (8, own))
    for k in range(nf):
        out[classes + 8 + k : classes + 9 + k, :] = right[:, k * own : (k + 1) * own]


def slot_kernel_part(par, parents_per_group, own):
    group = par.astype(I32) // parents_per_group
    groups = iota((16, own), 0)
    hot = group == groups
    earlier = (iota((own, own), 0) < iota((own, own), 1)).astype(F32).astype(BF16)
    ahead = jnp.dot(hot.astype(F32).astype(BF16), earlier, preferred_element_type=F32)
    start = jnp.sum((group < groups).astype(F32), axis=1, keepdims=True)
    return jnp.sum(jnp.where(hot, ahead + start, 0.0), axis=0, keepdims=True)


def placing(slot, own):
    return (iota((own, own), 0) == slot.astype(I32)).astype(F32).astype(BF16)


def sort_bins_kernel(nr, nf, parents_per_group, *refs):
    bins = refs[:nr]
    parents, out, slots = refs[nr:]
    own_feats, own = bins[0].shape[1:]
    copies = LANES // own_feats
    for j in range(nr):

        @pl.loop(0, nf)
        def _(k):
            slot = slot_kernel_part(parents[j, pl.ds(k, 1), :], parents_per_group, own)
            slots[j, pl.ds(k, 1), :] = slot
            block = jnp.concatenate([bins[j][k]] * copies, axis=0)
            placed = lax.dot_general(placing(slot, own), block, NT, preferred_element_type=F32)
            first = pl.multiple_of((j * nf + k) * own, TILE)
            out[pl.ds(first, own), :] = placed.astype(BF16)


def level_kernel(sizes, scal, offsets, near, far, parents, slots, bins, leaf, gains, totals, grads, mbins, mgrads, acc):
    nr, nf, ny, lo, hi, own, own_feats, classes, nodes = sizes
    blocks = nr * nf
    groups = nodes // GROUP_NODES
    half = GROUP_NODES * classes
    width = BINS * own_feats
    tiles = own // TILE
    me_feat = scal[0]
    leaf_t = leaf[...]
    label_row = hi * classes
    right_row = label_row + cdiv(hi, 8) * 8

    for jc, source in enumerate((near, far)):

        @pl.loop(0, ny * nf)
        def _(i):
            jy = i // nf
            jx = lax.rem(i, lo)
            jz = lax.rem(i // lo, hi)
            k = jnp.bitwise_xor(me_feat, jz * lo + jx)
            j = jy * 2 + jc
            yx = jy * lo + jx
            margins = source[yx, pl.ds(pl.multiple_of(jz * classes, 8), classes), :]
            label = source[yx, pl.ds(label_row + jz, 1), :]
            right = source[jy * lo, pl.ds(right_row + k, 1), :]
            for other in range(1, lo):
                right = right + source[jy * lo + other, pl.ds(right_row + k, 1), :]
            node = 2.0 * parents[j, pl.ds(k, 1), :] + right
            node_hot = (node == iota((nodes, own), 0).astype(F32)).astype(F32)
            moved = jnp.dot(leaf_t, node_hot, precision=lax.Precision.HIGHEST, preferred_element_type=F32)
            logits = margins + moved
            powers = jnp.exp(logits - jnp.max(logits, axis=0, keepdims=True))
            prob = powers / jnp.sum(powers, axis=0, keepdims=True)
            hot = label == iota((classes, own), 0).astype(F32)
            gradient = prob - jnp.where(hot, 1.0, 0.0)
            hessian = 2.0 * prob * (1.0 - prob)
            pad = jnp.broadcast_to(node, (LANES - 2 * classes, own))
            columns = jnp.concatenate([gradient, hessian, pad], axis=0).astype(BF16)
            slot = slots[j, pl.ds(k, 1), :]
            placed = lax.dot_general(placing(slot, own), columns, NT, preferred_element_type=F32)
            first = pl.multiple_of((j * nf + k) * own, TILE)
            grads[pl.ds(first, own), :] = placed.astype(BF16)

    acc[...] = jnp.zeros(acc.shape, F32)
    lane_bin = (iota((1, LANES), 1) // own_feats).astype(F32)
    bins_per = LANES // own_feats

    @pl.loop(0, groups)
    def _(q):
        def gather(block, place):
            begin = offsets[block, q]
            end = offsets[block, q + 1]
            t0 = begin // TILE
            count = jnp.where(end > begin, (end + TILE - 1) // TILE - t0, 0)
            base = block * tiles + t0

            @pl.loop(0, (count + COPY_TILES - 1) // COPY_TILES)
            def _(c):
                src = pl.multiple_of((base + c * COPY_TILES) * TILE, TILE)
                dst = pl.multiple_of((place + c * COPY_TILES) * TILE, TILE)
                rows = COPY_TILES * TILE
                mbins[pl.ds(dst, rows), :] = bins[pl.ds(src, rows), :]
                mgrads[pl.ds(dst, rows), :] = grads[pl.ds(src, rows), :]

            return place + count

        place = lax.fori_loop(0, blocks, gather, jnp.int32(0))
        tail = pl.multiple_of(place * TILE, TILE)
        mgrads[pl.ds(tail, CHUNK), :] = jnp.full((CHUNK, LANES), -1.0, BF16)

        @pl.loop(0, (place * TILE + CHUNK - 1) // CHUNK)
        def _(i):
            at = pl.multiple_of(i * CHUNK, CHUNK)
            columns = mgrads[pl.ds(at, CHUNK), :].T
            node = columns[2 * classes : 2 * classes + classes, :]
            parts = []
            for side in range(2):
                value = columns[side * classes : (side + 1) * classes, :]
                for n in range(GROUP_NODES):
                    wanted = (q * GROUP_NODES + n).astype(F32).astype(BF16)
                    parts.append(jnp.where(node == wanted, value, jnp.zeros_like(value)))
            weights = jnp.concatenate(parts, axis=0)
            value = (mbins[pl.ds(at, CHUNK), :].astype(F32) - lane_bin).astype(BF16)
            for m in range(width // COLS):
                below = []
                for s in range(COLS // LANES):
                    limit = (m * (COLS // LANES) + s) * bins_per
                    below.append(
                        jnp.where(value <= jnp.asarray(limit, BF16), jnp.asarray(1, BF16), jnp.asarray(0, BF16))
                    )
                below = jnp.concatenate(below, axis=1)
                span = slice(m * COLS, (m + 1) * COLS)
                acc[q, :, span] += jnp.dot(weights, below, preferred_element_type=F32)

        whole = acc[q, :, width - 1 : width]
        totals[q] = whole
        grad_whole = whole[:half]
        hess_whole = whole[half:]
        parent_score = grad_whole * grad_whole / (hess_whole + hess_ridge)
        for m in range(width // LANES):
            span = slice(m * LANES, (m + 1) * LANES)
            grad_left = acc[q, :half, span]
            hess_left = acc[q, half:, span]
            grad_right = grad_whole - grad_left
            hess_right = hess_whole - hess_left
            score = (
                grad_left * grad_left / (hess_left + hess_ridge)
                + grad_right * grad_right / (hess_right + hess_ridge)
                - parent_score
            )
            for n in range(GROUP_NODES):
                total = jnp.sum(score[n * classes : (n + 1) * classes], axis=0, keepdims=True)
                gains[q, n : n + 1, span] = total * (1.0 / classes)


def flip_by(value, index, count):
    step = 1
    while step < count:
        shaped = value.reshape((count // (2 * step), 2, step) + value.shape[1:])
        flipped = jnp.flip(shaped, axis=1)
        value = jnp.where((index // step) % 2 == 1, flipped, shaped).reshape(value.shape)
        step *= 2
    return value


def swap(value, axes, sizes, offsets):
    total = 1
    for size in sizes:
        total *= size
    flat = 0
    for size, offset in zip(sizes, offsets):
        flat = flat * size + offset
    return lax.ppermute(value, axes, [(i, i ^ flat) for i in range(total)])


def body(margins, labels, row_bins, parents, split_feature, split_bin, leaf_values):
    feat_dev, group_rows = row_bins.shape
    own, classes = margins.shape
    nodes = leaf_values.shape[0]
    parent_count = split_feature.shape[0]
    nf, nr = lax.axis_size("feat"), lax.axis_size("rows")
    feat, row = lax.axis_index("feat"), lax.axis_index("rows")
    own_feats = feat_dev // nr
    lo, ny = 2, nr // 2
    hi = nf // lo
    groups = nodes // GROUP_NODES
    parents_per_group = parent_count // groups
    blocks = nr * nf
    width = BINS * own_feats
    axes, sizes = ("rows", "feat"), (nr, nf)

    scal = jnp.concatenate([split_feature, split_bin, jnp.full((1,), feat * feat_dev, I32)])
    first_rows = classes + 8 + nf
    first = pl.pallas_call(
        functools.partial(first_message_kernel, parent_count, nf),
        out_shape=jax.ShapeDtypeStruct((first_rows, own), F32),
        in_specs=[SMEM] + [VMEM] * 4,
        out_specs=VMEM,
        name="first_message",
    )(scal, margins, labels.reshape(1, own), row_bins, parents.reshape(1, group_rows))

    along_z = [first] + [swap(first, axes, sizes, (0, lo * j)) for j in range(1, hi)]

    extra = cdiv(nf, own_feats)
    parent_rows = jnp.zeros((extra * own_feats, own), BF16).at[:nf].set(parents.reshape(nf, own).astype(BF16))
    parent_rows = jnp.broadcast_to(parent_rows.reshape(1, extra, own_feats, own), (nr, extra, own_feats, own))
    sent = row_bins.astype(BF16).reshape(nr, own_feats, nf, own).transpose(0, 2, 1, 3)
    sent = jnp.concatenate([sent, parent_rows], axis=1)
    bins_by = []
    for j in range(nr):
        piece = lax.dynamic_index_in_dim(sent, jnp.bitwise_xor(row, j), 0, keepdims=False)
        bins_by.append(piece if j == 0 else swap(piece, axes, sizes, (j, 0)))
    all_parents = jnp.stack([b[nf:].reshape(extra * own_feats, own)[:nf] for b in bins_by]).astype(F32)

    second = jnp.concatenate(
        [m[:classes] for m in along_z]
        + [m[classes : classes + 1] for m in along_z]
        + [jnp.zeros((cdiv(hi, 8) * 8 - hi, own), F32)]
        + [sum(m[classes + 8 :] for m in along_z)],
        axis=0,
    )
    plane = []
    for jy in range(ny):
        for jx in range(lo):
            plane.append(second if jy + jx == 0 else swap(second, axes, sizes, (2 * jy, jx)))
    near = jnp.stack(plane)
    far = swap(near, axes, sizes, (1, 0))

    placed_bins, slots = pl.pallas_call(
        functools.partial(sort_bins_kernel, nr, nf, parents_per_group),
        out_shape=(
            jax.ShapeDtypeStruct((blocks * own + COPY_TILES * TILE, LANES), BF16),
            jax.ShapeDtypeStruct((nr, nf, own), F32),
        ),
        in_specs=[VMEM] * (nr + 1),
        out_specs=(VMEM, VMEM),
        name="sort_bins",
    )(*bins_by, all_parents)

    group_of = all_parents.reshape(blocks, own).astype(I32) // parents_per_group
    offsets = jnp.stack([jnp.sum((group_of < q).astype(I32), axis=1) for q in range(groups + 1)], axis=1)

    shape = (nr, nf, ny, lo, hi, own, own_feats, classes, nodes)
    cap = blocks * own + CHUNK + COPY_TILES * TILE
    gains, totals = pl.pallas_call(
        functools.partial(level_kernel, shape),
        out_shape=(
            jax.ShapeDtypeStruct((groups, GROUP_NODES, width), F32),
            jax.ShapeDtypeStruct((groups, 2 * GROUP_NODES * classes, 1), F32),
        ),
        in_specs=[SMEM, SMEM] + [VMEM] * 6,
        out_specs=(VMEM, VMEM),
        scratch_shapes=[
            pltpu.VMEM((blocks * own + COPY_TILES * TILE, LANES), BF16),
            pltpu.VMEM((cap, LANES), BF16),
            pltpu.VMEM((cap, LANES), BF16),
            pltpu.VMEM((groups, 2 * GROUP_NODES * classes, width), F32),
        ],
        compiler_params=pltpu.CompilerParams(vmem_limit_bytes=60 * 2**20),
        name="level",
    )(feat.reshape(1), offsets, near, far, all_parents, slots, placed_bins, leaf_values.T)

    node_totals = totals.reshape(groups, 2, GROUP_NODES, classes).transpose(0, 2, 1, 3).reshape(nodes, 2 * classes)

    by_owner = gains.reshape(nr, nodes // nr, BINS, own_feats).transpose(0, 1, 3, 2)
    relative = flip_by(by_owner, row, nr)
    kept = jnp.stack(
        [relative[0]] + [swap(relative[j], axes, sizes, (j, 0)) for j in range(1, nr)]
    )
    split_gains = flip_by(kept, row, nr).transpose(1, 0, 2, 3).reshape(nodes // nr, feat_dev, BINS)
    return split_gains, node_totals


def solution(mesh):
    return jax.shard_map(
        body,
        mesh=mesh,
        in_specs=(
            P(("rows", "feat"), None),
            P(("rows", "feat")),
            P("feat", "rows"),
            P("rows"),
            P(),
            P(),
            P(),
        ),
        out_specs=(P("rows", "feat", None), P()),
        check_vma=False,
    )
```

```python
import functools

import jax
import jax.numpy as jnp
from jax import lax
from jax.experimental import pallas as pl
from jax.experimental.pallas import tpu as pltpu
from jax.sharding import PartitionSpec as P


BINS = 64
LANES = 128
TILE = 16
GROUP_NODES = 4
CHUNK = 512
COLS = 256
VMEM_SMALL = 12 * 2**20
VMEM_LARGE = 24 * 2**20
VMEM_WHOLE = 60 * 2**20


hess_ridge = 1.0

F32 = jnp.float32
BF16 = jnp.bfloat16
I32 = jnp.int32
NT = (((1,), (1,)), ((), ()))
VMEM = pl.BlockSpec(memory_space=pltpu.VMEM)
SMEM = pl.BlockSpec(memory_space=pltpu.SMEM)


def iota(shape, dim):
    return lax.broadcasted_iota(I32, shape, dim)


def first_kernel(nr, nf, *refs):
    sources = refs[:6]
    out = refs[6]
    sent = refs[7 : 7 + nr]
    held = refs[7 + nr : 13 + nr]
    sems = refs[13 + nr]
    copies = [pltpu.make_async_copy(source, here, sems.at[i]) for i, (source, here) in enumerate(zip(sources, held))]
    for copy in copies:
        copy.start()
    split_feature, split_bin, margins, labels, bins, parents = held
    classes, own = margins.shape
    feat_dev = bins.shape[0]
    own_feats = feat_dev // nr
    feat = lax.axis_index("feat")
    base = feat * feat_dev
    row = lax.axis_index("rows")
    for copy in copies:
        copy.wait()
    par = parents[...]
    cuts = [slice(k * own, (k + 1) * own) for k in range(nf)]
    par_rows = jnp.concatenate([par[:, cut] for cut in cuts], axis=0).astype(F32).astype(BF16)
    for j in range(nr):
        first = pl.multiple_of(jnp.bitwise_xor(row, j) * own_feats, own_feats)
        for k, cut in enumerate(cuts):
            piece = bins[pl.ds(first, own_feats), cut]
            sent[j][k * own_feats : (k + 1) * own_feats, :] = piece.astype(F32).astype(BF16)
        sent[j][nf * own_feats :, :] = par_rows
    out[0:classes, :] = margins[...]
    right = jnp.zeros(par.shape, F32)
    for p in range(split_feature.shape[0]):
        local = split_feature[p] - base
        owned = jnp.logical_and(local >= 0, local < feat_dev)
        threshold = jnp.where(owned, split_bin[p], BINS)
        deciding = bins[pl.ds(jnp.clip(local, 0, feat_dev - 1), 1), :]
        right = right + jnp.where((par == p) & (deciding > threshold), 1.0, 0.0)
    label = 2.0 * labels[...].astype(F32).reshape(1, own)
    mine = iota((nf, own), 0) == feat
    out[classes:, :] = jnp.concatenate([right[:, cut] for cut in cuts], axis=0) + jnp.where(mine, label, 0.0)


def plan_kernel(groups, parents_per_group, spare, parents, slots, where, chunks):
    blocks, own = parents.shape
    group = parents[...].astype(I32) // parents_per_group
    hot = [(group == q).astype(F32) for q in range(groups)]
    earlier = (iota((own, own), 0) < iota((own, own), 1)).astype(F32).astype(BF16)
    ahead = jnp.dot(jnp.concatenate(hot, axis=0).astype(BF16), earlier, preferred_element_type=F32)
    lane = iota((blocks, LANES), 1)
    used = jnp.zeros((blocks, 1), I32)
    counts, starts = [], []
    slot = jnp.zeros((blocks, own), F32)
    table = jnp.zeros((blocks, LANES), I32)
    for q in range(groups):
        rows = jnp.sum(hot[q], axis=1, keepdims=True).astype(I32)
        counts.append((rows + TILE - 1) // TILE)
        starts.append(used)
        first = (used * TILE).astype(F32)
        slot = slot + hot[q] * (ahead[q * blocks : (q + 1) * blocks] + first)
        table = table + jnp.where(lane == q, counts[q], 0)
        used = used + counts[q]
    slots[...] = slot
    above = (iota((blocks, blocks), 1) < iota((blocks, blocks), 0)).astype(F32).astype(BF16)
    before = jnp.dot(above, table.astype(F32).astype(BF16), preferred_element_type=F32).astype(I32)
    region = jnp.zeros((1, 1), I32)
    place = jnp.where(lane >= used, spare, 0)
    row8 = iota((8, LANES), 0)
    lane8 = iota((8, LANES), 1)
    spans = jnp.zeros((8, LANES), I32)
    per_chunk = CHUNK // TILE
    for q in range(groups):
        inside = (lane >= starts[q]) & (lane < starts[q] + counts[q])
        at = region * per_chunk + before[:, q : q + 1] + lane - starts[q]
        place = place + jnp.where(inside, at, 0)
        total = jnp.sum(counts[q], axis=0, keepdims=True)
        length = (total + per_chunk - 1) // per_chunk
        spans = spans + jnp.where((lane8 == q) & (row8 == 0), region, 0)
        spans = spans + jnp.where((lane8 == q) & (row8 == 1), length, 0)
        region = region + length
    where[...] = place
    chunks[...] = spans


def put_block(values, slot, tiles, where, block, out):
    own = values.shape[1]
    hot = (iota((tiles * TILE, own), 0) == slot.astype(I32)).astype(F32).astype(BF16)
    placed = lax.dot_general(hot, values, NT, preferred_element_type=F32).astype(BF16)
    for t in range(tiles):
        to = pl.multiple_of(where[block, t] * TILE, TILE)
        out[pl.ds(to, TILE), :] = placed[t * TILE : (t + 1) * TILE]


def sort_bins_kernel(nr, nf, tiles, unroll, where, *refs):
    bins = refs[:nr]
    slots, out = refs[nr:]
    own_feats = (bins[0].shape[0] - nf) // nf
    copies = LANES // own_feats
    for j in range(nr):

        @pl.loop(0, nf // unroll)
        def _(i):
            for u in range(unroll):
                k = i * unroll + u
                block = j * nf + k
                values = bins[j][pl.ds(pl.multiple_of(k * own_feats, own_feats), own_feats), :]
                values = jnp.concatenate([values] * copies, axis=0)
                put_block(values, slots[pl.ds(block, 1), :], tiles, where, block, out)


def put_grads(sizes, jc, where, source, parents, slots, leaf, grads):
    _, nf, ny, lo, hi, own, _, classes, nodes, tiles = sizes
    me_feat = lax.axis_index("feat")
    code_row = hi * classes
    rest = leaf[...]
    leaf_parts = []
    for _ in range(3):
        leaf_parts.append(rest.astype(BF16))
        rest = rest - leaf_parts[-1].astype(F32)
    leaf_parts = jnp.concatenate(leaf_parts, axis=1)
    grads[...] = jnp.zeros(grads.shape, BF16)

    @pl.loop(0, ny)
    def _(jy):
        j = jy * 2 + jc
        for jx, jz in [(jx, jz) for jx in range(lo) for jz in range(hi)]:
            yx = jy * lo + jx
            k = jnp.bitwise_xor(me_feat, jz * lo + jx)
            block = j * nf + k
            margins = source[yx, jz * classes : (jz + 1) * classes, :]
            code = source[jy * lo, pl.ds(code_row + k, 1), :]
            for other in range(1, lo):
                code = code + source[jy * lo + other, pl.ds(code_row + k, 1), :]
            label = jnp.floor(code * 0.5)
            right = code - 2.0 * label
            node = 2.0 * parents[pl.ds(block, 1), :] + right
            node_hot = (node == iota((nodes, own), 0).astype(F32)).astype(F32).astype(BF16)
            moved = jnp.dot(leaf_parts, jnp.concatenate([node_hot] * 3, axis=0), preferred_element_type=F32)
            logits = margins + moved
            powers = jnp.exp(logits - jnp.max(logits, axis=0, keepdims=True))
            prob = powers / jnp.sum(powers, axis=0, keepdims=True)
            hot = label == iota((classes, own), 0).astype(F32)
            gradient = prob - jnp.where(hot, 1.0, 0.0)
            hessian = 2.0 * prob * (1.0 - prob)
            pad = jnp.broadcast_to(node, (LANES - 2 * classes, own))
            columns = jnp.concatenate([gradient, hessian, pad], axis=0).astype(BF16)
            put_block(columns, slots[pl.ds(block, 1), :], tiles, where, block, grads)


def near_kernel(sizes, where, near, parents, slots, leaf, grads):
    put_grads(sizes, 0, where, near, parents, slots, leaf, grads)


def level_kernel(sizes, where, chunks, near_grads, far, parents, slots, bins, leaf, gains, totals, grads, acc):
    _, _, _, _, _, _, own_feats, classes, nodes, _ = sizes
    groups = nodes // GROUP_NODES
    half = GROUP_NODES * classes
    width = BINS * own_feats
    put_grads(sizes, 1, where, far, parents, slots, leaf, grads)
    lane_bin = (iota((1, LANES), 1) // own_feats).astype(F32)
    bins_per = LANES // own_feats

    @pl.loop(0, groups)
    def _(q):
        first = chunks[0, q]

        @pl.when(chunks[1, q] == 0)
        def _():
            acc[q] = jnp.zeros(acc.shape[1:], F32)

        @pl.loop(0, chunks[1, q])
        def _(i):
            at = pl.multiple_of((first + i) * CHUNK, CHUNK)
            columns = (near_grads[pl.ds(at, CHUNK), :] + grads[pl.ds(at, CHUNK), :]).T
            node = columns[2 * classes : 2 * classes + classes, :]
            parts = []
            for side in range(2):
                value = columns[side * classes : (side + 1) * classes, :]
                for n in range(GROUP_NODES):
                    wanted = (q * GROUP_NODES + n).astype(F32).astype(BF16)
                    parts.append(jnp.where(node == wanted, value, jnp.zeros_like(value)))
            weights = jnp.concatenate(parts, axis=0)
            value = (bins[pl.ds(at, CHUNK), :].astype(F32) - lane_bin).astype(BF16)
            for m in range(width // COLS):
                below = []
                for s in range(COLS // LANES):
                    limit = (m * (COLS // LANES) + s) * bins_per
                    below.append(
                        jnp.where(value <= jnp.asarray(limit, BF16), jnp.asarray(1, BF16), jnp.asarray(0, BF16))
                    )
                below = jnp.concatenate(below, axis=1)
                span = slice(m * COLS, (m + 1) * COLS)
                so_far = jnp.where(i == 0, 0.0, acc[q, :, span])
                acc[q, :, span] = so_far + jnp.dot(weights, below, preferred_element_type=F32)

        whole = acc[q, :, width - 1 : width]
        totals[q] = whole
        grad_whole = whole[:half]
        hess_whole = whole[half:]
        parent_score = grad_whole * grad_whole / (hess_whole + hess_ridge)
        for m in range(width // LANES):
            span = slice(m * LANES, (m + 1) * LANES)
            grad_left = acc[q, :half, span]
            hess_left = acc[q, half:, span]
            grad_right = grad_whole - grad_left
            hess_right = hess_whole - hess_left
            score = (
                grad_left * grad_left / (hess_left + hess_ridge)
                + grad_right * grad_right / (hess_right + hess_ridge)
                - parent_score
            )
            for n in range(GROUP_NODES):
                total = jnp.sum(score[n * classes : (n + 1) * classes], axis=0, keepdims=True)
                gains[q, n : n + 1, span] = total * (1.0 / classes)


def flip_by(value, index, count):
    step = 1
    while step < count:
        shaped = value.reshape((count // (2 * step), 2, step) + value.shape[1:])
        flipped = jnp.flip(shaped, axis=1)
        value = jnp.where((index // step) % 2 == 1, flipped, shaped).reshape(value.shape)
        step *= 2
    return value


def swap(value, axes, sizes, offsets):
    total = 1
    for size in sizes:
        total *= size
    flat = 0
    for size, offset in zip(sizes, offsets):
        flat = flat * size + offset
    return lax.ppermute(value, axes, [(i, i ^ flat) for i in range(total)])


def body(margins, labels, row_bins, parents, split_feature, split_bin, leaf_values):
    feat_dev, group_rows = row_bins.shape
    own, classes = margins.shape
    nodes = leaf_values.shape[0]
    parent_count = split_feature.shape[0]
    nf, nr = lax.axis_size("feat"), lax.axis_size("rows")
    row = lax.axis_index("rows")
    own_feats = feat_dev // nr
    lo, ny = 2, nr // 2
    hi = nf // lo
    groups = nodes // GROUP_NODES
    blocks = nr * nf
    width = BINS * own_feats
    axes, sizes = ("rows", "feat"), (nr, nf)

    message_rows = nf * own_feats + nf
    first_inputs = (split_feature, split_bin, margins.T, labels, row_bins, parents.reshape(1, group_rows))
    first, *sent = pl.pallas_call(
        functools.partial(first_kernel, nr, nf),
        out_shape=[jax.ShapeDtypeStruct((classes + nf, own), F32)]
        + [jax.ShapeDtypeStruct((message_rows, own), BF16)] * nr,
        in_specs=[pl.BlockSpec(memory_space=pltpu.HBM)] * 6,
        out_specs=[VMEM] * (nr + 1),
        scratch_shapes=[pltpu.SMEM(x.shape, x.dtype) for x in first_inputs[:2]]
        + [pltpu.VMEM(x.shape, x.dtype) for x in first_inputs[2:]]
        + [pltpu.SemaphoreType.DMA((6,))],
        compiler_params=pltpu.CompilerParams(vmem_limit_bytes=VMEM_WHOLE),
        name="first",
    )(*first_inputs)

    bins_by = [sent[0]]
    for j in range(1, nr):
        bins_by.append(swap(sent[j], axes, sizes, (j, 0)))
    along_z = [first] + [swap(first, axes, sizes, (0, lo * j)) for j in range(1, hi)]

    all_parents = jnp.concatenate([b[nf * own_feats :] for b in bins_by]).astype(F32)

    second = jnp.concatenate([m[:classes] for m in along_z] + [sum(m[classes:] for m in along_z)], axis=0)
    plane = []
    for jy in range(ny):
        for jx in range(lo):
            plane.append(second if jy + jx == 0 else swap(second, axes, sizes, (2 * jy, jx)))
    near = jnp.stack(plane)
    far = swap(near, axes, sizes, (1, 0))

    tiles = own // TILE + groups * (TILE - 1) // TILE
    spare = blocks * tiles + groups * (CHUNK // TILE - 1)
    ordered_rows = (spare + 1) * TILE
    slots, where, chunks = pl.pallas_call(
        functools.partial(plan_kernel, groups, parent_count // groups, spare),
        out_shape=(
            jax.ShapeDtypeStruct((blocks, own), F32),
            jax.ShapeDtypeStruct((blocks, LANES), I32),
            jax.ShapeDtypeStruct((8, LANES), I32),
        ),
        in_specs=[VMEM],
        out_specs=(VMEM,) * 3,
        compiler_params=pltpu.CompilerParams(vmem_limit_bytes=VMEM_SMALL),
        name="plan",
    )(all_parents)

    ordered_bins = pl.pallas_call(
        functools.partial(sort_bins_kernel, nr, nf, tiles, 8),
        out_shape=jax.ShapeDtypeStruct((ordered_rows, LANES), BF16),
        in_specs=[SMEM] + [VMEM] * (nr + 1),
        out_specs=VMEM,
        compiler_params=pltpu.CompilerParams(vmem_limit_bytes=VMEM_SMALL),
        name="sort_bins",
    )(where, *bins_by, slots)

    shape = (nr, nf, ny, lo, hi, own, own_feats, classes, nodes, tiles)
    leaf_t = leaf_values.T
    near_grads = pl.pallas_call(
        functools.partial(near_kernel, shape),
        out_shape=jax.ShapeDtypeStruct((ordered_rows, LANES), BF16),
        in_specs=[SMEM] + [VMEM] * 4,
        out_specs=VMEM,
        compiler_params=pltpu.CompilerParams(vmem_limit_bytes=VMEM_SMALL),
        name="near",
    )(where, near, all_parents, slots, leaf_t)

    gains, totals = pl.pallas_call(
        functools.partial(level_kernel, shape),
        out_shape=(
            jax.ShapeDtypeStruct((groups, GROUP_NODES, width), F32),
            jax.ShapeDtypeStruct((groups, 2 * GROUP_NODES * classes, 1), F32),
        ),
        in_specs=[SMEM] * 2 + [VMEM] * 6,
        out_specs=(VMEM, VMEM),
        scratch_shapes=[
            pltpu.VMEM((ordered_rows, LANES), BF16),
            pltpu.VMEM((groups, 2 * GROUP_NODES * classes, width), F32),
        ],
        compiler_params=pltpu.CompilerParams(vmem_limit_bytes=VMEM_LARGE),
        name="level",
    )(where, chunks, near_grads, far, all_parents, slots, ordered_bins, leaf_t)

    node_totals = totals.reshape(groups, 2, GROUP_NODES, classes).transpose(0, 2, 1, 3).reshape(nodes, 2 * classes)

    kept_nodes = nodes // nr
    relative = flip_by(gains.reshape(nr, kept_nodes, width), row, nr)
    kept = [relative[0]] + [swap(relative[j], axes, sizes, (j, 0)) for j in range(1, nr)]
    kept = flip_by(jnp.stack(kept), row, nr).reshape(nr, kept_nodes, BINS, own_feats)
    split_gains = kept.transpose(1, 0, 3, 2).reshape(kept_nodes, feat_dev, BINS)
    return split_gains, node_totals


def solution(mesh):
    return jax.shard_map(
        body,
        mesh=mesh,
        in_specs=(
            P(("rows", "feat"), None),
            P(("rows", "feat")),
            P("feat", "rows"),
            P("rows"),
            P(),
            P(),
            P(),
        ),
        out_specs=(P("rows", "feat", None), P()),
        check_vma=False,
    )
```

```python
import functools

import jax
import jax.numpy as jnp
from jax import lax
from jax.experimental import pallas as pl
from jax.experimental.pallas import tpu as pltpu
from jax.sharding import PartitionSpec as P


BINS = 64
LANES = 128
TILE = 16
GROUP_NODES = 4
CHUNK = 256
PIECES = (2048, 1024, 512, 256)
COLS = 256
VMEM_SMALL = 12 * 2**20
VMEM_MORE = 6 * 2**20
VMEM_WHOLE = 60 * 2**20


hess_ridge = 1.0

F32 = jnp.float32
BF16 = jnp.bfloat16
I32 = jnp.int32
NT = (((1,), (1,)), ((), ()))
VMEM = pl.BlockSpec(memory_space=pltpu.VMEM)
SMEM = pl.BlockSpec(memory_space=pltpu.SMEM)


def iota(shape, dim):
    return lax.broadcasted_iota(I32, shape, dim)


def first_kernel(nr, nf, *refs):
    sources = refs[:6]
    out = refs[6]
    sent = refs[7 : 7 + nr]
    held = refs[7 + nr : 13 + nr]
    sems = refs[13 + nr]
    copies = [pltpu.make_async_copy(source, here, sems.at[i]) for i, (source, here) in enumerate(zip(sources, held))]
    for copy in copies:
        copy.start()
    split_feature, split_bin, margins, labels, bins, parents = held
    classes, own = margins.shape
    feat_dev = bins.shape[0]
    own_feats = feat_dev // nr
    feat = lax.axis_index("feat")
    base = feat * feat_dev
    row = lax.axis_index("rows")
    for copy in copies:
        copy.wait()
    par = parents[...]
    cuts = [slice(k * own, (k + 1) * own) for k in range(nf)]
    par_rows = jnp.concatenate([par[:, cut] for cut in cuts], axis=0).astype(F32).astype(BF16)
    for j in range(nr):
        first = pl.multiple_of(jnp.bitwise_xor(row, j) * own_feats, own_feats)
        for k, cut in enumerate(cuts):
            piece = bins[pl.ds(first, own_feats), cut]
            sent[j][k * own_feats : (k + 1) * own_feats, :] = piece.astype(F32).astype(BF16)
        sent[j][nf * own_feats :, :] = par_rows
    out[0:classes, :] = margins[...]
    right = jnp.zeros(par.shape, F32)
    for p in range(split_feature.shape[0]):
        local = split_feature[p] - base
        owned = jnp.logical_and(local >= 0, local < feat_dev)
        threshold = jnp.where(owned, split_bin[p], BINS)
        deciding = bins[pl.ds(jnp.clip(local, 0, feat_dev - 1), 1), :]
        right = right + jnp.where((par == p) & (deciding > threshold), 1.0, 0.0)
    label = 2.0 * labels[...].astype(F32).reshape(1, own)
    mine = iota((nf, own), 0) == feat
    out[classes:, :] = jnp.concatenate([right[:, cut] for cut in cuts], axis=0) + jnp.where(mine, label, 0.0)


def plan_kernel(groups, parents_per_group, spare, parents, slots, where, chunks):
    blocks, own = parents.shape
    group = parents[...].astype(I32) // parents_per_group
    hot = [(group == q).astype(F32) for q in range(groups)]
    earlier = (iota((own, own), 0) < iota((own, own), 1)).astype(F32).astype(BF16)
    ahead = jnp.dot(jnp.concatenate(hot, axis=0).astype(BF16), earlier, preferred_element_type=F32)
    lane = iota((blocks, LANES), 1)
    used = jnp.zeros((blocks, 1), I32)
    counts, starts = [], []
    slot = jnp.zeros((blocks, own), F32)
    table = jnp.zeros((blocks, LANES), I32)
    for q in range(groups):
        rows = jnp.sum(hot[q], axis=1, keepdims=True).astype(I32)
        counts.append((rows + TILE - 1) // TILE)
        starts.append(used)
        first = (used * TILE).astype(F32)
        slot = slot + hot[q] * (ahead[q * blocks : (q + 1) * blocks] + first)
        table = table + jnp.where(lane == q, counts[q], 0)
        used = used + counts[q]
    slots[...] = slot
    above = (iota((blocks, blocks), 1) < iota((blocks, blocks), 0)).astype(F32).astype(BF16)
    before = jnp.dot(above, table.astype(F32).astype(BF16), preferred_element_type=F32).astype(I32)
    region = jnp.zeros((1, 1), I32)
    place = jnp.where(lane >= used, spare, 0)
    row8 = iota((8, LANES), 0)
    lane8 = iota((8, LANES), 1)
    spans = jnp.zeros((8, LANES), I32)
    per_chunk = CHUNK // TILE
    for q in range(groups):
        inside = (lane >= starts[q]) & (lane < starts[q] + counts[q])
        at = region * per_chunk + before[:, q : q + 1] + lane - starts[q]
        place = place + jnp.where(inside, at, 0)
        total = jnp.sum(counts[q], axis=0, keepdims=True)
        length = (total + per_chunk - 1) // per_chunk
        spans = spans + jnp.where((lane8 == q) & (row8 == 0), region, 0)
        spans = spans + jnp.where((lane8 == q) & (row8 == 1), length, 0)
        region = region + length
    where[...] = place
    chunks[...] = spans


def put_block(values, slot, tiles, where, block, out):
    own = values.shape[1]
    hot = (iota((tiles * TILE, own), 0) == slot.astype(I32)).astype(F32).astype(BF16)
    placed = lax.dot_general(hot, values, NT, preferred_element_type=F32).astype(BF16)
    for t in range(tiles):
        to = pl.multiple_of(where[block, t] * TILE, TILE)
        out[pl.ds(to, TILE), :] = placed[t * TILE : (t + 1) * TILE]


def sort_bins_kernel(nr, nf, tiles, unroll, where, *refs):
    bins = refs[:nr]
    slots, out = refs[nr:]
    own_feats = (bins[0].shape[0] - nf) // nf
    copies = LANES // own_feats
    for j in range(nr):

        @pl.loop(0, nf // unroll)
        def _(i):
            for u in range(unroll):
                k = i * unroll + u
                block = j * nf + k
                values = bins[j][pl.ds(pl.multiple_of(k * own_feats, own_feats), own_feats), :]
                values = jnp.concatenate([values] * copies, axis=0)
                put_block(values, slots[pl.ds(block, 1), :], tiles, where, block, out)


def put_grads(sizes, jc, where, source, parents, slots, leaf, grads):
    _, nf, ny, lo, hi, own, _, classes, nodes, tiles = sizes
    me_feat = lax.axis_index("feat")
    code_row = hi * classes
    rest = leaf[...]
    leaf_parts = []
    for _ in range(3):
        leaf_parts.append(rest.astype(BF16))
        rest = rest - leaf_parts[-1].astype(F32)
    leaf_parts = jnp.concatenate(leaf_parts, axis=1)
    grads[...] = jnp.zeros(grads.shape, BF16)

    @pl.loop(0, ny)
    def _(jy):
        j = jy * 2 + jc
        for jx, jz in [(jx, jz) for jx in range(lo) for jz in range(hi)]:
            yx = jy * lo + jx
            k = jnp.bitwise_xor(me_feat, jz * lo + jx)
            block = j * nf + k
            margins = source[yx, jz * classes : (jz + 1) * classes, :]
            code = source[jy * lo, pl.ds(code_row + k, 1), :]
            for other in range(1, lo):
                code = code + source[jy * lo + other, pl.ds(code_row + k, 1), :]
            label = jnp.floor(code * 0.5)
            right = code - 2.0 * label
            node = 2.0 * parents[pl.ds(block, 1), :] + right
            node_hot = (node == iota((nodes, own), 0).astype(F32)).astype(F32).astype(BF16)
            moved = jnp.dot(leaf_parts, jnp.concatenate([node_hot] * 3, axis=0), preferred_element_type=F32)
            logits = margins + moved
            powers = jnp.exp(logits - jnp.max(logits, axis=0, keepdims=True))
            prob = powers / jnp.sum(powers, axis=0, keepdims=True)
            hot = label == iota((classes, own), 0).astype(F32)
            gradient = prob - jnp.where(hot, 1.0, 0.0)
            hessian = 2.0 * prob * (1.0 - prob)
            member = node - GROUP_NODES * jnp.floor(node * (1.0 / GROUP_NODES))
            parts = [jnp.where(member == n, v, 0.0) for v in (gradient, hessian) for n in range(GROUP_NODES)]
            columns = jnp.concatenate(parts, axis=0).astype(BF16)
            put_block(columns, slots[pl.ds(block, 1), :], tiles, where, block, grads)


def near_kernel(sizes, where, near, parents, slots, leaf, grads):
    put_grads(sizes, 0, where, near, parents, slots, leaf, grads)


def level_kernel(sizes, where, chunks, near_grads, far, parents, slots, bins, leaf, gains, totals, grads, acc):
    _, _, _, _, _, _, own_feats, classes, nodes, _ = sizes
    groups = nodes // GROUP_NODES
    half = GROUP_NODES * classes
    width = BINS * own_feats
    put_grads(sizes, 1, where, far, parents, slots, leaf, grads)
    bins_per = LANES // own_feats
    lane_bin = (iota((1, LANES), 1) // own_feats).astype(F32)
    one, none = jnp.asarray(1, BF16), jnp.asarray(0, BF16)
    member = (iota((8, half), 1) // classes == iota((8, half), 0)).astype(F32)
    member = jnp.concatenate([member] * 3, axis=1).astype(BF16)

    @pl.loop(0, groups)
    def _(q):
        first = chunks[0, q]

        @pl.when(chunks[1, q] == 0)
        def _():
            acc[q] = jnp.zeros(acc.shape[1:], F32)

        def add_rows(at, rows):
            at = pl.multiple_of(at * CHUNK, CHUNK)
            fresh = at == first * CHUNK
            columns = near_grads[pl.ds(at, rows), :] + grads[pl.ds(at, rows), :]
            value = (bins[pl.ds(at, rows), :].astype(F32) - lane_bin).astype(BF16).T
            for m in range(width // COLS):
                below = []
                for s in range(COLS // LANES):
                    limit = (m * (COLS // LANES) + s) * bins_per
                    below.append(jnp.where(value <= jnp.asarray(limit, BF16), one, none))
                below = jnp.concatenate(below, axis=0)
                span = slice(m * COLS, (m + 1) * COLS)
                so_far = jnp.where(fresh, 0.0, acc[q, span, :])
                acc[q, span, :] = so_far + jnp.dot(below, columns, preferred_element_type=F32)

        length = chunks[1, q]
        largest = PIECES[0] // CHUNK

        @pl.loop(0, length // largest)
        def _(i):
            add_rows(first + i * largest, PIECES[0])

        for rows in PIECES[1:]:
            units = rows // CHUNK

            @pl.when((length // units) % 2 == 1)
            def _():
                add_rows(first + length // (2 * units) * (2 * units), rows)

        whole = acc[q, width - 1 : width, :]
        totals[q] = whole
        grad_whole = whole[:, :half]
        hess_whole = whole[:, half:]
        parent_score = grad_whole * grad_whole / (hess_whole + hess_ridge)
        for m in range(width // LANES):
            span = slice(m * LANES, (m + 1) * LANES)
            grad_left = acc[q, span, :half]
            hess_left = acc[q, span, half:]
            grad_right = grad_whole - grad_left
            hess_right = hess_whole - hess_left
            rest = (
                grad_left * grad_left / (hess_left + hess_ridge)
                + grad_right * grad_right / (hess_right + hess_ridge)
                - parent_score
            )
            parts = []
            for _ in range(3):
                parts.append(rest.astype(BF16))
                rest = rest - parts[-1].astype(F32)
            parts = jnp.concatenate(parts, axis=1)
            total = lax.dot_general(member, parts, NT, preferred_element_type=F32)
            gains[q, :, span] = total[:GROUP_NODES] * (1.0 / classes)


def flip_by(value, index, count):
    step = 1
    while step < count:
        shaped = value.reshape((count // (2 * step), 2, step) + value.shape[1:])
        flipped = jnp.flip(shaped, axis=1)
        value = jnp.where((index // step) % 2 == 1, flipped, shaped).reshape(value.shape)
        step *= 2
    return value


def swap(value, axes, sizes, offsets):
    total = 1
    for size in sizes:
        total *= size
    flat = 0
    for size, offset in zip(sizes, offsets):
        flat = flat * size + offset
    return lax.ppermute(value, axes, [(i, i ^ flat) for i in range(total)])


def body(margins, labels, row_bins, parents, split_feature, split_bin, leaf_values):
    feat_dev, group_rows = row_bins.shape
    own, classes = margins.shape
    nodes = leaf_values.shape[0]
    parent_count = split_feature.shape[0]
    nf, nr = lax.axis_size("feat"), lax.axis_size("rows")
    row = lax.axis_index("rows")
    own_feats = feat_dev // nr
    lo, ny = 2, nr // 2
    hi = nf // lo
    groups = nodes // GROUP_NODES
    blocks = nr * nf
    width = BINS * own_feats
    axes, sizes = ("rows", "feat"), (nr, nf)

    message_rows = nf * own_feats + nf
    first_inputs = (split_feature, split_bin, margins.T, labels, row_bins, parents.reshape(1, group_rows))
    first, *sent = pl.pallas_call(
        functools.partial(first_kernel, nr, nf),
        out_shape=[jax.ShapeDtypeStruct((classes + nf, own), F32)]
        + [jax.ShapeDtypeStruct((message_rows, own), BF16)] * nr,
        in_specs=[pl.BlockSpec(memory_space=pltpu.HBM)] * 6,
        out_specs=[VMEM] * (nr + 1),
        scratch_shapes=[pltpu.SMEM(x.shape, x.dtype) for x in first_inputs[:2]]
        + [pltpu.VMEM(x.shape, x.dtype) for x in first_inputs[2:]]
        + [pltpu.SemaphoreType.DMA((6,))],
        compiler_params=pltpu.CompilerParams(vmem_limit_bytes=VMEM_WHOLE),
        name="first",
    )(*first_inputs)

    bins_by = [sent[0]]
    for j in range(1, nr):
        bins_by.append(swap(sent[j], axes, sizes, (j, 0)))
    along_z = [first] + [swap(first, axes, sizes, (0, lo * j)) for j in range(1, hi)]

    all_parents = jnp.concatenate([b[nf * own_feats :] for b in bins_by]).astype(F32)

    second = jnp.concatenate([m[:classes] for m in along_z] + [sum(m[classes:] for m in along_z)], axis=0)
    plane = []
    for jy in range(ny):
        for jx in range(lo):
            plane.append(second if jy + jx == 0 else swap(second, axes, sizes, (2 * jy, jx)))
    near = jnp.stack(plane)
    far = swap(near, axes, sizes, (1, 0))

    tiles = own // TILE + groups * (TILE - 1) // TILE
    spare = blocks * tiles + groups * (CHUNK // TILE - 1)
    ordered_rows = (spare + 1) * TILE
    slots, where, chunks = pl.pallas_call(
        functools.partial(plan_kernel, groups, parent_count // groups, spare),
        out_shape=(
            jax.ShapeDtypeStruct((blocks, own), F32),
            jax.ShapeDtypeStruct((blocks, LANES), I32),
            jax.ShapeDtypeStruct((8, LANES), I32),
        ),
        in_specs=[VMEM],
        out_specs=(VMEM,) * 3,
        compiler_params=pltpu.CompilerParams(vmem_limit_bytes=VMEM_SMALL),
        name="plan",
    )(all_parents)

    ordered_bins = pl.pallas_call(
        functools.partial(sort_bins_kernel, nr, nf, tiles, 8),
        out_shape=jax.ShapeDtypeStruct((ordered_rows, LANES), BF16),
        in_specs=[SMEM] + [VMEM] * (nr + 1),
        out_specs=VMEM,
        compiler_params=pltpu.CompilerParams(vmem_limit_bytes=VMEM_SMALL),
        name="sort_bins",
    )(where, *bins_by, slots)

    columns = 2 * GROUP_NODES * classes
    level_bytes = ordered_rows * 2 * (2 * columns + LANES) + groups * width * columns * 4 + VMEM_MORE
    near_bytes = ordered_rows * 2 * columns + VMEM_MORE
    shape = (nr, nf, ny, lo, hi, own, own_feats, classes, nodes, tiles)
    leaf_t = leaf_values.T
    near_grads = pl.pallas_call(
        functools.partial(near_kernel, shape),
        out_shape=jax.ShapeDtypeStruct((ordered_rows, columns), BF16),
        in_specs=[SMEM] + [VMEM] * 4,
        out_specs=VMEM,
        compiler_params=pltpu.CompilerParams(vmem_limit_bytes=near_bytes),
        name="near",
    )(where, near, all_parents, slots, leaf_t)

    gains, totals = pl.pallas_call(
        functools.partial(level_kernel, shape),
        out_shape=(
            jax.ShapeDtypeStruct((groups, GROUP_NODES, width), F32),
            jax.ShapeDtypeStruct((groups, 1, columns), F32),
        ),
        in_specs=[SMEM] * 2 + [VMEM] * 6,
        out_specs=(VMEM, VMEM),
        scratch_shapes=[
            pltpu.VMEM((ordered_rows, columns), BF16),
            pltpu.VMEM((groups, width, columns), F32),
        ],
        compiler_params=pltpu.CompilerParams(vmem_limit_bytes=level_bytes),
        name="level",
    )(where, chunks, near_grads, far, all_parents, slots, ordered_bins, leaf_t)

    node_totals = totals.reshape(groups, 2, GROUP_NODES, classes).transpose(0, 2, 1, 3).reshape(nodes, 2 * classes)

    kept_nodes = nodes // nr
    relative = flip_by(gains.reshape(nr, kept_nodes, width), row, nr)
    kept = [relative[0]] + [swap(relative[j], axes, sizes, (j, 0)) for j in range(1, nr)]
    kept = flip_by(jnp.stack(kept), row, nr).reshape(nr, kept_nodes, BINS, own_feats)
    split_gains = kept.transpose(1, 0, 3, 2).reshape(kept_nodes, feat_dev, BINS)
    return split_gains, node_totals


def solution(mesh):
    return jax.shard_map(
        body,
        mesh=mesh,
        in_specs=(
            P(("rows", "feat"), None),
            P(("rows", "feat")),
            P("feat", "rows"),
            P("rows"),
            P(),
            P(),
            P(),
        ),
        out_specs=(P("rows", "feat", None), P()),
        check_vma=False,
    )
```

```python
import functools

import jax
import jax.numpy as jnp
from jax import lax
from jax.experimental import pallas as pl
from jax.experimental.pallas import tpu as pltpu
from jax.sharding import PartitionSpec as P


BINS = 64
LANES = 128
TILE = 16
GROUP_NODES = 4
CHUNK = 256
SUB = 256
PIECES = (2048, 1024, 512, 256)
COLS = 256
VMEM_SMALL = 12 * 2**20
VMEM_MORE = 6 * 2**20
VMEM_WHOLE = 60 * 2**20


hess_ridge = 1.0

F32 = jnp.float32
BF16 = jnp.bfloat16
I32 = jnp.int32
NT = (((1,), (1,)), ((), ()))
VMEM = pl.BlockSpec(memory_space=pltpu.VMEM)
SMEM = pl.BlockSpec(memory_space=pltpu.SMEM)


def iota(shape, dim):
    return lax.broadcasted_iota(I32, shape, dim)


def put_bins(bins, parents, cuts, out):
    own_feats = bins.shape[0]
    for k, cut in enumerate(cuts):
        out[k * own_feats : (k + 1) * own_feats, :] = bins[:, cut].astype(F32).astype(BF16)
    out[len(cuts) * own_feats :, :] = jnp.concatenate([parents[:, cut] for cut in cuts], axis=0).astype(F32).astype(BF16)


def own_kernel(nf, bins, parents, out, held, sem):
    own_feats = held.shape[0]
    own = held.shape[1] // nf
    at = pl.multiple_of(lax.axis_index("rows") * own_feats, own_feats)
    copy = pltpu.make_async_copy(bins.at[pl.ds(at, own_feats), :], held, sem)
    copy.start()
    copy.wait()
    put_bins(held[...], parents[...], [slice(k * own, (k + 1) * own) for k in range(nf)], out)


def first_kernel(nr, nf, *refs):
    sources = refs[:6]
    out = refs[6]
    sent = refs[7 : 6 + nr]
    held = refs[6 + nr : 12 + nr]
    sems = refs[12 + nr]
    copies = [pltpu.make_async_copy(source, here, sems.at[i]) for i, (source, here) in enumerate(zip(sources, held))]
    for copy in copies:
        copy.start()
    split_feature, split_bin, margins, labels, bins, parents = held
    classes, own = margins.shape
    feat_dev = bins.shape[0]
    own_feats = feat_dev // nr
    feat = lax.axis_index("feat")
    base = feat * feat_dev
    row = lax.axis_index("rows")
    for copy in copies:
        copy.wait()
    par = parents[...]
    cuts = [slice(k * own, (k + 1) * own) for k in range(nf)]
    for j in range(1, nr):
        at = pl.multiple_of(jnp.bitwise_xor(row, j) * own_feats, own_feats)
        put_bins(bins[pl.ds(at, own_feats), :], par, cuts, sent[j - 1])
    out[0:classes, :] = margins[...]
    right = jnp.zeros(par.shape, F32)
    for p in range(split_feature.shape[0]):
        local = split_feature[p] - base
        owned = jnp.logical_and(local >= 0, local < feat_dev)
        threshold = jnp.where(owned, split_bin[p], BINS)
        deciding = bins[pl.ds(jnp.clip(local, 0, feat_dev - 1), 1), :]
        right = right + jnp.where((par == p) & (deciding > threshold), 1.0, 0.0)
    label = 2.0 * labels[...].astype(F32).reshape(1, own)
    mine = iota((nf, own), 0) == feat
    out[classes:, :] = jnp.concatenate([right[:, cut] for cut in cuts], axis=0) + jnp.where(mine, label, 0.0)


def cut_pair(pair, sub):
    joined = jnp.concatenate(pair, axis=1)
    return [joined[:, at : at + sub] for at in range(0, joined.shape[1], sub)]


def plan_kernel(groups, parents_per_group, spare, nr, nf, lo, sub, given, slots, where, chunks):
    feat = lax.axis_index("feat")
    parents = []
    for j in range(nr):
        for far in range(0, nf, lo):
            pair = [given[pl.ds(j * nf + jnp.bitwise_xor(feat, far + x), 1), :] for x in range(lo)]
            parents += cut_pair(pair, sub)
    parents = jnp.concatenate(parents, axis=0)
    blocks, own = parents.shape
    group = parents.astype(I32) // parents_per_group
    hot = [(group == q).astype(F32) for q in range(groups)]
    earlier = (iota((own, own), 0) < iota((own, own), 1)).astype(F32).astype(BF16)
    ahead = jnp.dot(jnp.concatenate(hot, axis=0).astype(BF16), earlier, preferred_element_type=F32)
    lane = iota((blocks, LANES), 1)
    used = jnp.zeros((blocks, 1), I32)
    counts, starts = [], []
    slot = jnp.zeros((blocks, own), F32)
    table = jnp.zeros((blocks, LANES), I32)
    for q in range(groups):
        rows = jnp.sum(hot[q], axis=1, keepdims=True).astype(I32)
        counts.append((rows + TILE - 1) // TILE)
        starts.append(used)
        first = (used * TILE).astype(F32)
        slot = slot + hot[q] * (ahead[q * blocks : (q + 1) * blocks] + first)
        table = table + jnp.where(lane == q, counts[q], 0)
        used = used + counts[q]
    slots[...] = slot
    above = (iota((blocks, blocks), 1) < iota((blocks, blocks), 0)).astype(F32).astype(BF16)
    before = jnp.dot(above, table.astype(F32).astype(BF16), preferred_element_type=F32).astype(I32)
    region = jnp.zeros((1, 1), I32)
    place = jnp.where(lane >= used, spare, 0)
    row8 = iota((8, LANES), 0)
    lane8 = iota((8, LANES), 1)
    spans = jnp.zeros((8, LANES), I32)
    per_chunk = CHUNK // TILE
    for q in range(groups):
        inside = (lane >= starts[q]) & (lane < starts[q] + counts[q])
        at = region * per_chunk + before[:, q : q + 1] + lane - starts[q]
        place = place + jnp.where(inside, at, 0)
        total = jnp.sum(counts[q], axis=0, keepdims=True)
        length = (total + per_chunk - 1) // per_chunk
        spans = spans + jnp.where((lane8 == q) & (row8 == 0), region, 0)
        spans = spans + jnp.where((lane8 == q) & (row8 == 1), length, 0)
        region = region + length
    where[...] = place
    chunks[...] = spans


def put_block(values, slot, tiles, where, block, out):
    own = values.shape[1]
    hot = (iota((tiles * TILE, own), 0) == slot.astype(I32)).astype(F32).astype(BF16)
    placed = lax.dot_general(hot, values, NT, preferred_element_type=F32).astype(BF16)
    for t in range(tiles):
        to = pl.multiple_of(where[block, t] * TILE, TILE)
        out[pl.ds(to, TILE), :] = placed[t * TILE : (t + 1) * TILE]


def sort_bins_kernel(nr, nf, lo, sub, tiles, unroll, where, *refs):
    bins = refs[:nr]
    slots, out = refs[nr:]
    own_feats = (bins[0].shape[0] - nf) // nf
    copies = LANES // own_feats
    cuts = slots.shape[0] * lo // (nr * nf)
    feat = lax.axis_index("feat")
    for j in range(nr):

        @pl.loop(0, nf // (lo * unroll))
        def _(i):
            for u in range(unroll):
                jz = i * unroll + u
                pair = []
                for jx in range(lo):
                    k = jnp.bitwise_xor(feat, jz * lo + jx)
                    pair.append(bins[j][pl.ds(pl.multiple_of(k * own_feats, own_feats), own_feats), :])
                for c, values in enumerate(cut_pair(pair, sub)):
                    part = (j * (nf // lo) + jz) * cuts + c
                    values = jnp.concatenate([values] * copies, axis=0)
                    put_block(values, slots[pl.ds(part, 1), :], tiles, where, part, out)


def put_grads(sizes, jc, where, source, parents, slots, leaf, grads):
    _, nf, ny, lo, hi, own, _, classes, nodes, tiles, sub = sizes
    me_feat = lax.axis_index("feat")
    code_row = hi * classes
    rest = leaf[...]
    leaf_parts = []
    for _ in range(3):
        leaf_parts.append(rest.astype(BF16))
        rest = rest - leaf_parts[-1].astype(F32)
    leaf_parts = jnp.concatenate(leaf_parts, axis=1)
    grads[...] = jnp.zeros(grads.shape, BF16)

    @pl.loop(0, ny)
    def _(jy):
        j = jy * 2 + jc
        pair = []
        for jz, jx in [(jz, jx) for jz in range(hi) for jx in range(lo)]:
            yx = jy * lo + jx
            k = jnp.bitwise_xor(me_feat, jz * lo + jx)
            block = j * nf + k
            margins = source[yx, jz * classes : (jz + 1) * classes, :]
            code = source[jy * lo, pl.ds(code_row + k, 1), :]
            for other in range(1, lo):
                code = code + source[jy * lo + other, pl.ds(code_row + k, 1), :]
            label = jnp.floor(code * 0.5)
            right = code - 2.0 * label
            node = 2.0 * parents[pl.ds(block, 1), :] + right
            node_hot = (node == iota((nodes, own), 0).astype(F32)).astype(F32).astype(BF16)
            moved = jnp.dot(leaf_parts, jnp.concatenate([node_hot] * 3, axis=0), preferred_element_type=F32)
            logits = margins + moved
            powers = jnp.exp(logits - jnp.max(logits, axis=0, keepdims=True))
            prob = powers / jnp.sum(powers, axis=0, keepdims=True)
            hot = label == iota((classes, own), 0).astype(F32)
            gradient = prob - jnp.where(hot, 1.0, 0.0)
            hessian = 2.0 * prob * (1.0 - prob)
            member = node - GROUP_NODES * jnp.floor(node * (1.0 / GROUP_NODES))
            parts = [jnp.where(member == n, v, 0.0) for v in (gradient, hessian) for n in range(GROUP_NODES)]
            pair.append(jnp.concatenate(parts, axis=0).astype(BF16))
            if jx < lo - 1:
                continue
            cuts = cut_pair(pair, sub)
            pair = []
            for c, columns in enumerate(cuts):
                part = (j * hi + jz) * len(cuts) + c
                put_block(columns, slots[pl.ds(part, 1), :], tiles, where, part, grads)


def near_kernel(sizes, where, near, parents, slots, leaf, grads):
    put_grads(sizes, 0, where, near, parents, slots, leaf, grads)


def level_kernel(sizes, where, chunks, near_grads, far, parents, slots, bins, leaf, gains, totals, grads, acc):
    _, _, _, _, _, _, own_feats, classes, nodes, _, _ = sizes
    groups = nodes // GROUP_NODES
    half = GROUP_NODES * classes
    width = BINS * own_feats
    put_grads(sizes, 1, where, far, parents, slots, leaf, grads)
    bins_per = LANES // own_feats
    lane_bin = (iota((1, LANES), 1) // own_feats).astype(F32)
    one, none = jnp.asarray(1, BF16), jnp.asarray(0, BF16)
    member = (iota((8, half), 1) // classes == iota((8, half), 0)).astype(F32)
    member = jnp.concatenate([member] * 3, axis=1).astype(BF16)

    @pl.loop(0, groups)
    def _(q):
        first = chunks[0, q]

        @pl.when(chunks[1, q] == 0)
        def _():
            acc[q] = jnp.zeros(acc.shape[1:], F32)

        def add_rows(at, rows):
            at = pl.multiple_of(at * CHUNK, CHUNK)
            fresh = at == first * CHUNK
            columns = near_grads[pl.ds(at, rows), :] + grads[pl.ds(at, rows), :]
            value = (bins[pl.ds(at, rows), :].astype(F32) - lane_bin).astype(BF16).T
            for m in range(width // COLS):
                below = []
                for s in range(COLS // LANES):
                    limit = (m * (COLS // LANES) + s) * bins_per
                    below.append(jnp.where(value <= jnp.asarray(limit, BF16), one, none))
                below = jnp.concatenate(below, axis=0)
                span = slice(m * COLS, (m + 1) * COLS)
                so_far = jnp.where(fresh, 0.0, acc[q, span, :])
                acc[q, span, :] = so_far + jnp.dot(below, columns, preferred_element_type=F32)

        length = chunks[1, q]
        largest = PIECES[0] // CHUNK

        @pl.loop(0, length // largest)
        def _(i):
            add_rows(first + i * largest, PIECES[0])

        for rows in PIECES[1:]:
            units = rows // CHUNK

            @pl.when((length // units) % 2 == 1)
            def _():
                add_rows(first + length // (2 * units) * (2 * units), rows)

        whole = acc[q, width - 1 : width, :]
        totals[q] = whole
        grad_whole = whole[:, :half]
        hess_whole = whole[:, half:]
        parent_score = grad_whole * grad_whole / (hess_whole + hess_ridge)
        for m in range(width // LANES):
            span = slice(m * LANES, (m + 1) * LANES)
            grad_left = acc[q, span, :half]
            hess_left = acc[q, span, half:]
            grad_right = grad_whole - grad_left
            hess_right = hess_whole - hess_left
            rest = (
                grad_left * grad_left / (hess_left + hess_ridge)
                + grad_right * grad_right / (hess_right + hess_ridge)
                - parent_score
            )
            parts = []
            for _ in range(3):
                parts.append(rest.astype(BF16))
                rest = rest - parts[-1].astype(F32)
            parts = jnp.concatenate(parts, axis=1)
            total = lax.dot_general(member, parts, NT, preferred_element_type=F32)
            gains[q, :, span] = total[:GROUP_NODES] * (1.0 / classes)


def flip_by(value, index, count):
    step = 1
    while step < count:
        shaped = value.reshape((count // (2 * step), 2, step) + value.shape[1:])
        flipped = jnp.flip(shaped, axis=1)
        value = jnp.where((index // step) % 2 == 1, flipped, shaped).reshape(value.shape)
        step *= 2
    return value


def swap(value, axes, sizes, offsets):
    total = 1
    for size in sizes:
        total *= size
    flat = 0
    for size, offset in zip(sizes, offsets):
        flat = flat * size + offset
    return lax.ppermute(value, axes, [(i, i ^ flat) for i in range(total)])


def body(margins, labels, row_bins, parents, split_feature, split_bin, leaf_values):
    feat_dev, group_rows = row_bins.shape
    own, classes = margins.shape
    nodes = leaf_values.shape[0]
    parent_count = split_feature.shape[0]
    nf, nr = lax.axis_size("feat"), lax.axis_size("rows")
    row = lax.axis_index("rows")
    own_feats = feat_dev // nr
    lo, ny = 2, nr // 2
    hi = nf // lo
    groups = nodes // GROUP_NODES
    blocks = nr * nf
    width = BINS * own_feats
    axes, sizes = ("rows", "feat"), (nr, nf)

    message_rows = nf * own_feats + nf
    first_inputs = (split_feature, split_bin, margins.T, labels, row_bins, parents.reshape(1, group_rows))
    first, *sent = pl.pallas_call(
        functools.partial(first_kernel, nr, nf),
        out_shape=[jax.ShapeDtypeStruct((classes + nf, own), F32)]
        + [jax.ShapeDtypeStruct((message_rows, own), BF16)] * (nr - 1),
        in_specs=[pl.BlockSpec(memory_space=pltpu.HBM)] * 6,
        out_specs=[VMEM] * nr,
        scratch_shapes=[pltpu.SMEM(x.shape, x.dtype) for x in first_inputs[:2]]
        + [pltpu.VMEM(x.shape, x.dtype) for x in first_inputs[2:]]
        + [pltpu.SemaphoreType.DMA((6,))],
        compiler_params=pltpu.CompilerParams(vmem_limit_bytes=VMEM_WHOLE),
        name="first",
    )(*first_inputs)

    own_bins = pl.pallas_call(
        functools.partial(own_kernel, nf),
        out_shape=jax.ShapeDtypeStruct((message_rows, own), BF16),
        in_specs=[pl.BlockSpec(memory_space=pltpu.HBM), VMEM],
        out_specs=VMEM,
        scratch_shapes=[pltpu.VMEM((own_feats, group_rows), I32), pltpu.SemaphoreType.DMA],
        compiler_params=pltpu.CompilerParams(vmem_limit_bytes=VMEM_SMALL),
        name="own_bins",
    )(row_bins, parents.reshape(1, group_rows))
    bins_by = [own_bins]
    for j in range(1, nr):
        bins_by.append(swap(sent[j - 1], axes, sizes, (j, 0)))
    along_z = [first] + [swap(first, axes, sizes, (0, lo * j)) for j in range(1, hi)]

    all_parents = jnp.concatenate([b[nf * own_feats :] for b in bins_by]).astype(F32)

    second = jnp.concatenate([m[:classes] for m in along_z] + [sum(m[classes:] for m in along_z)], axis=0)
    plane = []
    for jy in range(ny):
        for jx in range(lo):
            plane.append(second if jy + jx == 0 else swap(second, axes, sizes, (2 * jy, jx)))
    near = jnp.stack(plane)
    far = swap(near, axes, sizes, (1, 0))

    sub = SUB if lo * own % SUB == 0 else own
    parts = blocks * own // sub
    tiles = sub // TILE + groups * (TILE - 1) // TILE
    spare = parts * tiles + groups * (CHUNK // TILE - 1)
    ordered_rows = (spare + 1) * TILE
    slots, where, chunks = pl.pallas_call(
        functools.partial(plan_kernel, groups, parent_count // groups, spare, nr, nf, lo, sub),
        out_shape=(
            jax.ShapeDtypeStruct((parts, sub), F32),
            jax.ShapeDtypeStruct((parts, LANES), I32),
            jax.ShapeDtypeStruct((8, LANES), I32),
        ),
        in_specs=[VMEM],
        out_specs=(VMEM,) * 3,
        compiler_params=pltpu.CompilerParams(vmem_limit_bytes=VMEM_SMALL),
        name="plan",
    )(all_parents)

    ordered_bins = pl.pallas_call(
        functools.partial(sort_bins_kernel, nr, nf, lo, sub, tiles, 2),
        out_shape=jax.ShapeDtypeStruct((ordered_rows, LANES), BF16),
        in_specs=[SMEM] + [VMEM] * (nr + 1),
        out_specs=VMEM,
        compiler_params=pltpu.CompilerParams(vmem_limit_bytes=VMEM_SMALL),
        name="sort_bins",
    )(where, *bins_by, slots)

    columns = 2 * GROUP_NODES * classes
    level_bytes = ordered_rows * 2 * (2 * columns + LANES) + groups * width * columns * 4 + VMEM_MORE
    near_bytes = ordered_rows * 2 * columns + VMEM_MORE
    shape = (nr, nf, ny, lo, hi, own, own_feats, classes, nodes, tiles, sub)
    leaf_t = leaf_values.T
    near_grads = pl.pallas_call(
        functools.partial(near_kernel, shape),
        out_shape=jax.ShapeDtypeStruct((ordered_rows, columns), BF16),
        in_specs=[SMEM] + [VMEM] * 4,
        out_specs=VMEM,
        compiler_params=pltpu.CompilerParams(vmem_limit_bytes=near_bytes),
        name="near",
    )(where, near, all_parents, slots, leaf_t)

    gains, totals = pl.pallas_call(
        functools.partial(level_kernel, shape),
        out_shape=(
            jax.ShapeDtypeStruct((groups, GROUP_NODES, width), F32),
            jax.ShapeDtypeStruct((groups, 1, columns), F32),
        ),
        in_specs=[SMEM] * 2 + [VMEM] * 6,
        out_specs=(VMEM, VMEM),
        scratch_shapes=[
            pltpu.VMEM((ordered_rows, columns), BF16),
            pltpu.VMEM((groups, width, columns), F32),
        ],
        compiler_params=pltpu.CompilerParams(vmem_limit_bytes=level_bytes),
        name="level",
    )(where, chunks, near_grads, far, all_parents, slots, ordered_bins, leaf_t)

    node_totals = totals.reshape(groups, 2, GROUP_NODES, classes).transpose(0, 2, 1, 3).reshape(nodes, 2 * classes)

    kept_nodes = nodes // nr
    relative = flip_by(gains.reshape(nr, kept_nodes, width), row, nr)
    kept = [relative[0]] + [swap(relative[j], axes, sizes, (j, 0)) for j in range(1, nr)]
    kept = flip_by(jnp.stack(kept), row, nr).reshape(nr, kept_nodes, BINS, own_feats)
    split_gains = kept.transpose(1, 0, 3, 2).reshape(kept_nodes, feat_dev, BINS)
    return split_gains, node_totals


def solution(mesh):
    return jax.shard_map(
        body,
        mesh=mesh,
        in_specs=(
            P(("rows", "feat"), None),
            P(("rows", "feat")),
            P("feat", "rows"),
            P("rows"),
            P(),
            P(),
            P(),
        ),
        out_specs=(P("rows", "feat", None), P()),
        check_vma=False,
    )
```

```python
import functools

import jax
import jax.numpy as jnp
from jax import lax
from jax.experimental import pallas as pl
from jax.experimental.pallas import tpu as pltpu
from jax.sharding import PartitionSpec as P


BINS = 64
LANES = 128
TILE = 16
GROUP_NODES = 4
CHUNK = 256
SUB = 256
PIECES = (2048, 1024, 512, 256)
COLS = 256
VMEM_SMALL = 12 * 2**20
VMEM_MORE = 6 * 2**20
VMEM_WHOLE = 60 * 2**20


hess_ridge = 1.0

F32 = jnp.float32
BF16 = jnp.bfloat16
I32 = jnp.int32
NT = (((1,), (1,)), ((), ()))
VMEM = pl.BlockSpec(memory_space=pltpu.VMEM)
SMEM = pl.BlockSpec(memory_space=pltpu.SMEM)


def iota(shape, dim):
    return lax.broadcasted_iota(I32, shape, dim)


def put_bins(bins, parents, cuts, out):
    own_feats = bins.shape[0]
    for k, cut in enumerate(cuts):
        out[k * own_feats : (k + 1) * own_feats, :] = bins[:, cut].astype(F32).astype(BF16)
    out[len(cuts) * own_feats :, :] = jnp.concatenate([parents[:, cut] for cut in cuts], axis=0).astype(F32).astype(BF16)


def own_kernel(nf, bins, parents, out, held, sem):
    own_feats = held.shape[0]
    own = held.shape[1] // nf
    at = pl.multiple_of(lax.axis_index("rows") * own_feats, own_feats)
    copy = pltpu.make_async_copy(bins.at[pl.ds(at, own_feats), :], held, sem)
    copy.start()
    copy.wait()
    put_bins(held[...], parents[...], [slice(k * own, (k + 1) * own) for k in range(nf)], out)


def first_kernel(nr, nf, *refs):
    sources = refs[:6]
    out = refs[6]
    sent = refs[7 : 6 + nr]
    held = refs[6 + nr : 12 + nr]
    sems = refs[12 + nr]
    copies = [pltpu.make_async_copy(source, here, sems.at[i]) for i, (source, here) in enumerate(zip(sources, held))]
    for copy in copies:
        copy.start()
    split_feature, split_bin, margins, labels, bins, parents = held
    classes, own = margins.shape
    feat_dev = bins.shape[0]
    own_feats = feat_dev // nr
    feat = lax.axis_index("feat")
    base = feat * feat_dev
    row = lax.axis_index("rows")
    for copy in copies:
        copy.wait()
    par = parents[...]
    cuts = [slice(k * own, (k + 1) * own) for k in range(nf)]
    for j in range(1, nr):
        at = pl.multiple_of(jnp.bitwise_xor(row, j) * own_feats, own_feats)
        put_bins(bins[pl.ds(at, own_feats), :], par, cuts, sent[j - 1])
    out[0:classes, :] = margins[...]
    right = jnp.zeros(par.shape, F32)
    for p in range(split_feature.shape[0]):
        local = split_feature[p] - base
        owned = jnp.logical_and(local >= 0, local < feat_dev)
        threshold = jnp.where(owned, split_bin[p], BINS)
        deciding = bins[pl.ds(jnp.clip(local, 0, feat_dev - 1), 1), :]
        right = right + jnp.where((par == p) & (deciding > threshold), 1.0, 0.0)
    label = 2.0 * labels[...].astype(F32).reshape(1, own)
    mine = iota((nf, own), 0) == feat
    out[classes:, :] = jnp.concatenate([right[:, cut] for cut in cuts], axis=0) + jnp.where(mine, label, 0.0)


def each(count, limit, step):
    if count <= limit:
        for i in range(count):
            step(i)
    else:
        pl.loop(0, count)(step)


def cut_pair(pair, sub):
    joined = jnp.concatenate(pair, axis=1)
    return [joined[:, at : at + sub] for at in range(0, joined.shape[1], sub)]


def plan_kernel(groups, parents_per_group, spare, nr, nf, lo, sub, given, slots, where, chunks):
    feat = lax.axis_index("feat")
    parents = []
    for j in range(nr):
        for far in range(0, nf, lo):
            pair = [given[pl.ds(j * nf + jnp.bitwise_xor(feat, far + x), 1), :] for x in range(lo)]
            parents += cut_pair(pair, sub)
    parents = jnp.concatenate(parents, axis=0)
    blocks, own = parents.shape
    group = parents.astype(I32) // parents_per_group
    hot = [(group == q).astype(F32) for q in range(groups)]
    earlier = (iota((own, own), 0) < iota((own, own), 1)).astype(F32).astype(BF16)
    ahead = jnp.dot(jnp.concatenate(hot, axis=0).astype(BF16), earlier, preferred_element_type=F32)
    lane = iota((blocks, LANES), 1)
    used = jnp.zeros((blocks, 1), I32)
    counts, starts = [], []
    slot = jnp.zeros((blocks, own), F32)
    table = jnp.zeros((blocks, LANES), I32)
    for q in range(groups):
        rows = jnp.sum(hot[q], axis=1, keepdims=True).astype(I32)
        counts.append((rows + TILE - 1) // TILE)
        starts.append(used)
        first = (used * TILE).astype(F32)
        slot = slot + hot[q] * (ahead[q * blocks : (q + 1) * blocks] + first)
        table = table + jnp.where(lane == q, counts[q], 0)
        used = used + counts[q]
    slots[...] = slot
    above = (iota((blocks, blocks), 1) < iota((blocks, blocks), 0)).astype(F32).astype(BF16)
    before = jnp.dot(above, table.astype(F32).astype(BF16), preferred_element_type=F32).astype(I32)
    region = jnp.zeros((1, 1), I32)
    place = jnp.where(lane >= used, spare, 0)
    row8 = iota((8, LANES), 0)
    lane8 = iota((8, LANES), 1)
    spans = jnp.zeros((8, LANES), I32)
    per_chunk = CHUNK // TILE
    for q in range(groups):
        inside = (lane >= starts[q]) & (lane < starts[q] + counts[q])
        at = region * per_chunk + before[:, q : q + 1] + lane - starts[q]
        place = place + jnp.where(inside, at, 0)
        total = jnp.sum(counts[q], axis=0, keepdims=True)
        length = (total + per_chunk - 1) // per_chunk
        spans = spans + jnp.where((lane8 == q) & (row8 == 0), region, 0)
        spans = spans + jnp.where((lane8 == q) & (row8 == 1), length, 0)
        region = region + length
    where[...] = place * TILE
    chunks[...] = spans


def put_block(values, slot, tiles, where, block, out):
    own = values.shape[1]
    middle = tiles * TILE // 2
    line = (iota((tiles * TILE, own), 0) - middle).astype(F32).astype(BF16)
    wanted = jnp.broadcast_to(slot - middle, (tiles * TILE, own)).astype(BF16)
    hot = jnp.where(line == wanted, jnp.asarray(1, BF16), jnp.asarray(0, BF16))
    placed = lax.dot_general(hot, values, NT, preferred_element_type=F32).astype(BF16)
    places = [where[block, t] for t in range(tiles)]
    for t in range(tiles):
        to = pl.multiple_of(places[t], TILE)
        out[pl.ds(to, TILE), :] = placed[t * TILE : (t + 1) * TILE]


def sort_bins_kernel(nr, nf, lo, sub, tiles, where, *refs):
    bins = refs[:nr]
    slots, out = refs[nr:]
    own_feats = (bins[0].shape[0] - nf) // nf
    copies = LANES // own_feats
    cuts = slots.shape[0] * lo // (nr * nf)
    feat = lax.axis_index("feat")
    for j in range(nr):

        def sort_pair(jz):
            pair = []
            for jx in range(lo):
                k = jnp.bitwise_xor(feat, jz * lo + jx)
                pair.append(bins[j][pl.ds(pl.multiple_of(k * own_feats, own_feats), own_feats), :])
            for c, values in enumerate(cut_pair(pair, sub)):
                part = (j * (nf // lo) + jz) * cuts + c
                values = jnp.concatenate([values] * copies, axis=0)
                put_block(values, slots[pl.ds(part, 1), :], tiles, where, part, out)

        each(nf // lo, 4, sort_pair)


def put_grads(sizes, jc, where, source, parents, slots, leaf, grads):
    _, nf, ny, lo, hi, own, _, classes, nodes, tiles, sub = sizes
    me_feat = lax.axis_index("feat")
    code_row = hi * classes
    rest = leaf[...]
    leaf_parts = []
    for _ in range(3):
        leaf_parts.append(rest.astype(BF16))
        rest = rest - leaf_parts[-1].astype(F32)
    leaf_parts = jnp.concatenate(leaf_parts, axis=1)
    grads[...] = jnp.zeros(grads.shape, BF16)

    def put_rows(jy):
        j = jy * 2 + jc
        pair = []
        for jz, jx in [(jz, jx) for jz in range(hi) for jx in range(lo)]:
            yx = jy * lo + jx
            k = jnp.bitwise_xor(me_feat, jz * lo + jx)
            block = j * nf + k
            margins = source[yx, jz * classes : (jz + 1) * classes, :]
            code = source[jy * lo, pl.ds(code_row + k, 1), :]
            for other in range(1, lo):
                code = code + source[jy * lo + other, pl.ds(code_row + k, 1), :]
            label = jnp.floor(code * 0.5)
            right = code - 2.0 * label
            node = 2.0 * parents[pl.ds(block, 1), :] + right
            node_hot = (node == iota((nodes, own), 0).astype(F32)).astype(F32).astype(BF16)
            moved = jnp.dot(leaf_parts, jnp.concatenate([node_hot] * 3, axis=0), preferred_element_type=F32)
            logits = margins + moved
            powers = jnp.exp(logits - jnp.max(logits, axis=0, keepdims=True))
            prob = powers * (1.0 / jnp.sum(powers, axis=0, keepdims=True))
            hot = label == iota((classes, own), 0).astype(F32)
            gradient = prob - jnp.where(hot, 1.0, 0.0)
            hessian = 2.0 * prob * (1.0 - prob)
            member = node - GROUP_NODES * jnp.floor(node * (1.0 / GROUP_NODES))
            member = jnp.broadcast_to(member, (classes, own)).astype(BF16)
            none = jnp.zeros((classes, own), BF16)
            parts = []
            for value in (gradient.astype(BF16), hessian.astype(BF16)):
                parts += [jnp.where(member == jnp.asarray(n, BF16), value, none) for n in range(GROUP_NODES)]
            pair.append(jnp.concatenate(parts, axis=0))
            if jx < lo - 1:
                continue
            cuts = cut_pair(pair, sub)
            pair = []
            for c, columns in enumerate(cuts):
                part = (j * hi + jz) * len(cuts) + c
                put_block(columns, slots[pl.ds(part, 1), :], tiles, where, part, grads)

    each(ny, 2, put_rows)


def near_kernel(sizes, where, near, parents, slots, leaf, grads):
    put_grads(sizes, 0, where, near, parents, slots, leaf, grads)


def level_kernel(sizes, where, chunks, near_grads, far, parents, slots, bins, leaf, gains, totals, grads, acc):
    _, _, _, _, _, _, own_feats, classes, nodes, _, _ = sizes
    groups = nodes // GROUP_NODES
    half = GROUP_NODES * classes
    width = BINS * own_feats
    put_grads(sizes, 1, where, far, parents, slots, leaf, grads)
    bins_per = LANES // own_feats
    lane_bin = (iota((1, LANES), 1) // own_feats).astype(F32)
    one, none = jnp.asarray(1, BF16), jnp.asarray(0, BF16)
    member = (iota((8, half), 1) // classes == iota((8, half), 0)).astype(F32)
    member = jnp.concatenate([member] * 3, axis=1).astype(BF16)

    @pl.loop(0, groups)
    def _(q):
        first = chunks[0, q]

        @pl.when(chunks[1, q] == 0)
        def _():
            acc[q] = jnp.zeros(acc.shape[1:], F32)

        def add_rows(at, rows):
            at = pl.multiple_of(at * CHUNK, CHUNK)
            fresh = at == first * CHUNK
            columns = near_grads[pl.ds(at, rows), :] + grads[pl.ds(at, rows), :]
            value = (bins[pl.ds(at, rows), :].astype(F32) - lane_bin).astype(BF16).T
            for m in range(width // COLS):
                below = []
                for s in range(COLS // LANES):
                    limit = (m * (COLS // LANES) + s) * bins_per
                    below.append(jnp.where(value <= jnp.asarray(limit, BF16), one, none))
                below = jnp.concatenate(below, axis=0)
                span = slice(m * COLS, (m + 1) * COLS)
                so_far = jnp.where(fresh, 0.0, acc[q, span, :])
                acc[q, span, :] = so_far + jnp.dot(below, columns, preferred_element_type=F32)

        length = chunks[1, q]
        largest = PIECES[0] // CHUNK

        @pl.loop(0, length // largest)
        def _(i):
            add_rows(first + i * largest, PIECES[0])

        for rows in PIECES[1:]:
            units = rows // CHUNK

            @pl.when((length // units) % 2 == 1)
            def _():
                add_rows(first + length // (2 * units) * (2 * units), rows)

        whole = acc[q, width - 1 : width, :]
        totals[q] = whole
        grad_whole = whole[:, :half]
        hess_whole = whole[:, half:]
        parent_score = grad_whole * grad_whole / (hess_whole + hess_ridge)
        for m in range(width // LANES):
            span = slice(m * LANES, (m + 1) * LANES)
            grad_left = acc[q, span, :half]
            hess_left = acc[q, span, half:]
            grad_right = grad_whole - grad_left
            hess_right = hess_whole - hess_left
            rest = (
                grad_left * grad_left / (hess_left + hess_ridge)
                + grad_right * grad_right / (hess_right + hess_ridge)
                - parent_score
            )
            parts = []
            for _ in range(3):
                parts.append(rest.astype(BF16))
                rest = rest - parts[-1].astype(F32)
            parts = jnp.concatenate(parts, axis=1)
            total = lax.dot_general(member, parts, NT, preferred_element_type=F32)
            gains[q, :, span] = total[:GROUP_NODES] * (1.0 / classes)


def flip_by(value, index, count):
    step = 1
    while step < count:
        shaped = value.reshape((count // (2 * step), 2, step) + value.shape[1:])
        flipped = jnp.flip(shaped, axis=1)
        value = jnp.where((index // step) % 2 == 1, flipped, shaped).reshape(value.shape)
        step *= 2
    return value


def swap(value, axes, sizes, offsets):
    total = 1
    for size in sizes:
        total *= size
    flat = 0
    for size, offset in zip(sizes, offsets):
        flat = flat * size + offset
    return lax.ppermute(value, axes, [(i, i ^ flat) for i in range(total)])


def body(margins, labels, row_bins, parents, split_feature, split_bin, leaf_values):
    feat_dev, group_rows = row_bins.shape
    own, classes = margins.shape
    nodes = leaf_values.shape[0]
    parent_count = split_feature.shape[0]
    nf, nr = lax.axis_size("feat"), lax.axis_size("rows")
    row = lax.axis_index("rows")
    own_feats = feat_dev // nr
    lo, ny = 2, nr // 2
    hi = nf // lo
    groups = nodes // GROUP_NODES
    blocks = nr * nf
    width = BINS * own_feats
    axes, sizes = ("rows", "feat"), (nr, nf)

    message_rows = nf * own_feats + nf
    first_inputs = (split_feature, split_bin, margins.T, labels, row_bins, parents.reshape(1, group_rows))
    first, *sent = pl.pallas_call(
        functools.partial(first_kernel, nr, nf),
        out_shape=[jax.ShapeDtypeStruct((classes + nf, own), F32)]
        + [jax.ShapeDtypeStruct((message_rows, own), BF16)] * (nr - 1),
        in_specs=[pl.BlockSpec(memory_space=pltpu.HBM)] * 6,
        out_specs=[VMEM] * nr,
        scratch_shapes=[pltpu.SMEM(x.shape, x.dtype) for x in first_inputs[:2]]
        + [pltpu.VMEM(x.shape, x.dtype) for x in first_inputs[2:]]
        + [pltpu.SemaphoreType.DMA((6,))],
        compiler_params=pltpu.CompilerParams(vmem_limit_bytes=VMEM_WHOLE),
        name="first",
    )(*first_inputs)

    own_bins = pl.pallas_call(
        functools.partial(own_kernel, nf),
        out_shape=jax.ShapeDtypeStruct((message_rows, own), BF16),
        in_specs=[pl.BlockSpec(memory_space=pltpu.HBM), VMEM],
        out_specs=VMEM,
        scratch_shapes=[pltpu.VMEM((own_feats, group_rows), I32), pltpu.SemaphoreType.DMA],
        compiler_params=pltpu.CompilerParams(vmem_limit_bytes=VMEM_SMALL),
        name="own_bins",
    )(row_bins, parents.reshape(1, group_rows))
    bins_by = [own_bins]
    for j in range(1, nr):
        bins_by.append(swap(sent[j - 1], axes, sizes, (j, 0)))
    along_z = [first] + [swap(first, axes, sizes, (0, lo * j)) for j in range(1, hi)]

    all_parents = jnp.concatenate([b[nf * own_feats :] for b in bins_by]).astype(F32)

    second = jnp.concatenate([m[:classes] for m in along_z] + [sum(m[classes:] for m in along_z)], axis=0)
    plane = []
    for jy in range(ny):
        for jx in range(lo):
            plane.append(second if jy + jx == 0 else swap(second, axes, sizes, (2 * jy, jx)))
    near = jnp.stack(plane)
    far = swap(near, axes, sizes, (1, 0))

    sub = SUB if lo * own % SUB == 0 else own
    parts = blocks * own // sub
    tiles = sub // TILE + groups * (TILE - 1) // TILE
    spare = parts * tiles + groups * (CHUNK // TILE - 1)
    ordered_rows = (spare + 1) * TILE
    slots, where, chunks = pl.pallas_call(
        functools.partial(plan_kernel, groups, parent_count // groups, spare, nr, nf, lo, sub),
        out_shape=(
            jax.ShapeDtypeStruct((parts, sub), F32),
            jax.ShapeDtypeStruct((parts, LANES), I32),
            jax.ShapeDtypeStruct((8, LANES), I32),
        ),
        in_specs=[VMEM],
        out_specs=(VMEM,) * 3,
        compiler_params=pltpu.CompilerParams(vmem_limit_bytes=VMEM_SMALL),
        name="plan",
    )(all_parents)

    ordered_bins = pl.pallas_call(
        functools.partial(sort_bins_kernel, nr, nf, lo, sub, tiles),
        out_shape=jax.ShapeDtypeStruct((ordered_rows, LANES), BF16),
        in_specs=[SMEM] + [VMEM] * (nr + 1),
        out_specs=VMEM,
        compiler_params=pltpu.CompilerParams(vmem_limit_bytes=VMEM_SMALL),
        name="sort_bins",
    )(where, *bins_by, slots)

    columns = 2 * GROUP_NODES * classes
    level_bytes = ordered_rows * 2 * (2 * columns + LANES) + groups * width * columns * 4 + VMEM_MORE
    near_bytes = ordered_rows * 2 * columns + VMEM_MORE
    shape = (nr, nf, ny, lo, hi, own, own_feats, classes, nodes, tiles, sub)
    leaf_t = leaf_values.T
    near_grads = pl.pallas_call(
        functools.partial(near_kernel, shape),
        out_shape=jax.ShapeDtypeStruct((ordered_rows, columns), BF16),
        in_specs=[SMEM] + [VMEM] * 4,
        out_specs=VMEM,
        compiler_params=pltpu.CompilerParams(vmem_limit_bytes=near_bytes),
        name="near",
    )(where, near, all_parents, slots, leaf_t)

    gains, totals = pl.pallas_call(
        functools.partial(level_kernel, shape),
        out_shape=(
            jax.ShapeDtypeStruct((groups, GROUP_NODES, width), F32),
            jax.ShapeDtypeStruct((groups, 1, columns), F32),
        ),
        in_specs=[SMEM] * 2 + [VMEM] * 6,
        out_specs=(VMEM, VMEM),
        scratch_shapes=[
            pltpu.VMEM((ordered_rows, columns), BF16),
            pltpu.VMEM((groups, width, columns), F32),
        ],
        compiler_params=pltpu.CompilerParams(vmem_limit_bytes=level_bytes),
        name="level",
    )(where, chunks, near_grads, far, all_parents, slots, ordered_bins, leaf_t)

    node_totals = totals.reshape(groups, 2, GROUP_NODES, classes).transpose(0, 2, 1, 3).reshape(nodes, 2 * classes)

    kept_nodes = nodes // nr
    relative = flip_by(gains.reshape(nr, kept_nodes, width), row, nr)
    kept = [relative[0]] + [swap(relative[j], axes, sizes, (j, 0)) for j in range(1, nr)]
    kept = flip_by(jnp.stack(kept), row, nr).reshape(nr, kept_nodes, BINS, own_feats)
    split_gains = kept.transpose(1, 0, 3, 2).reshape(kept_nodes, feat_dev, BINS)
    return split_gains, node_totals


def solution(mesh):
    return jax.shard_map(
        body,
        mesh=mesh,
        in_specs=(
            P(("rows", "feat"), None),
            P(("rows", "feat")),
            P("feat", "rows"),
            P("rows"),
            P(),
            P(),
            P(),
        ),
        out_specs=(P("rows", "feat", None), P()),
        check_vma=False,
    )
```

```python
import functools

import jax
import jax.numpy as jnp
from jax import lax
from jax.experimental import pallas as pl
from jax.experimental.pallas import tpu as pltpu
from jax.sharding import PartitionSpec as P


BINS = 64
LANES = 128
TILE = 16
GROUP_NODES = 4
CHUNK = 256
SUB = 256
PIECES = (2048, 1024, 512, 256)
COLS = 256
VMEM_SMALL = 12 * 2**20
VMEM_MORE = 6 * 2**20
VMEM_WHOLE = 60 * 2**20


hess_ridge = 1.0

F32 = jnp.float32
BF16 = jnp.bfloat16
I32 = jnp.int32
NT = (((1,), (1,)), ((), ()))
VMEM = pl.BlockSpec(memory_space=pltpu.VMEM)
SMEM = pl.BlockSpec(memory_space=pltpu.SMEM)


def iota(shape, dim):
    return lax.broadcasted_iota(I32, shape, dim)


def put_bins(bins, parents, cuts, out):
    own_feats = bins.shape[0]
    for k, cut in enumerate(cuts):
        out[k * own_feats : (k + 1) * own_feats, :] = bins[:, cut].astype(F32).astype(BF16)
    out[len(cuts) * own_feats :, :] = jnp.concatenate([parents[:, cut] for cut in cuts], axis=0).astype(F32).astype(BF16)


def own_kernel(nf, bins, parents, out, held, sem):
    own_feats = held.shape[0]
    own = held.shape[1] // nf
    at = pl.multiple_of(lax.axis_index("rows") * own_feats, own_feats)
    copy = pltpu.make_async_copy(bins.at[pl.ds(at, own_feats), :], held, sem)
    copy.start()
    copy.wait()
    put_bins(held[...], parents[...], [slice(k * own, (k + 1) * own) for k in range(nf)], out)


def first_kernel(nr, nf, *refs):
    sources = refs[:6]
    out = refs[6]
    sent = refs[7 : 6 + nr]
    held = refs[6 + nr : 12 + nr]
    sems = refs[12 + nr]
    copies = [pltpu.make_async_copy(source, here, sems.at[i]) for i, (source, here) in enumerate(zip(sources, held))]
    for copy in copies:
        copy.start()
    split_feature, split_bin, margins, labels, bins, parents = held
    classes, own = margins.shape
    feat_dev = bins.shape[0]
    own_feats = feat_dev // nr
    feat = lax.axis_index("feat")
    base = feat * feat_dev
    row = lax.axis_index("rows")
    for copy in copies:
        copy.wait()
    par = parents[...]
    cuts = [slice(k * own, (k + 1) * own) for k in range(nf)]
    for j in range(1, nr):
        at = pl.multiple_of(jnp.bitwise_xor(row, j) * own_feats, own_feats)
        put_bins(bins[pl.ds(at, own_feats), :], par, cuts, sent[j - 1])
    out[0:classes, :] = margins[...]
    right = jnp.zeros(par.shape, F32)
    for p in range(split_feature.shape[0]):
        local = split_feature[p] - base
        owned = jnp.logical_and(local >= 0, local < feat_dev)
        threshold = jnp.where(owned, split_bin[p], BINS)
        deciding = bins[pl.ds(jnp.clip(local, 0, feat_dev - 1), 1), :]
        right = right + jnp.where((par == p) & (deciding > threshold), 1.0, 0.0)
    label = 2.0 * labels[...].astype(F32).reshape(1, own)
    mine = iota((nf, own), 0) == feat
    out[classes:, :] = jnp.concatenate([right[:, cut] for cut in cuts], axis=0) + jnp.where(mine, label, 0.0)


def each(count, limit, step):
    if count <= limit:
        for i in range(count):
            step(i)
    else:
        pl.loop(0, count)(step)


def cut_pair(pair, sub):
    joined = jnp.concatenate(pair, axis=1)
    return [joined[:, at : at + sub] for at in range(0, joined.shape[1], sub)]


def plan_kernel(groups, parents_per_group, spare, nr, nf, lo, sub, given, slots, where, chunks):
    feat = lax.axis_index("feat")
    parents = []
    for j in range(nr):
        for far in range(0, nf, lo):
            pair = [given[pl.ds(j * nf + jnp.bitwise_xor(feat, far + x), 1), :] for x in range(lo)]
            parents += cut_pair(pair, sub)
    parents = jnp.concatenate(parents, axis=0)
    blocks, own = parents.shape
    group = parents.astype(I32) // parents_per_group
    hot = [(group == q).astype(F32) for q in range(groups)]
    earlier = (iota((own, own), 0) < iota((own, own), 1)).astype(F32).astype(BF16)
    ahead = jnp.dot(jnp.concatenate(hot, axis=0).astype(BF16), earlier, preferred_element_type=F32)
    lane = iota((blocks, LANES), 1)
    used = jnp.zeros((blocks, 1), I32)
    counts, starts = [], []
    slot = jnp.zeros((blocks, own), F32)
    table = jnp.zeros((blocks, LANES), I32)
    for q in range(groups):
        rows = jnp.sum(hot[q], axis=1, keepdims=True).astype(I32)
        counts.append((rows + TILE - 1) // TILE)
        starts.append(used)
        first = (used * TILE).astype(F32)
        slot = slot + hot[q] * (ahead[q * blocks : (q + 1) * blocks] + first)
        table = table + jnp.where(lane == q, counts[q], 0)
        used = used + counts[q]
    slots[...] = slot
    above = (iota((blocks, blocks), 1) < iota((blocks, blocks), 0)).astype(F32).astype(BF16)
    before = jnp.dot(above, table.astype(F32).astype(BF16), preferred_element_type=F32).astype(I32)
    region = jnp.zeros((1, 1), I32)
    place = jnp.where(lane >= used, spare, 0)
    row8 = iota((8, LANES), 0)
    lane8 = iota((8, LANES), 1)
    spans = jnp.zeros((8, LANES), I32)
    per_chunk = CHUNK // TILE
    for q in range(groups):
        inside = (lane >= starts[q]) & (lane < starts[q] + counts[q])
        at = region * per_chunk + before[:, q : q + 1] + lane - starts[q]
        place = place + jnp.where(inside, at, 0)
        total = jnp.sum(counts[q], axis=0, keepdims=True)
        length = (total + per_chunk - 1) // per_chunk
        spans = spans + jnp.where((lane8 == q) & (row8 == 0), region, 0)
        spans = spans + jnp.where((lane8 == q) & (row8 == 1), length, 0)
        region = region + length
    where[...] = place * TILE
    chunks[...] = spans


def put_block(values, slot, tiles, where, block, out):
    own = values.shape[1]
    middle = tiles * TILE // 2
    line = (iota((tiles * TILE, own), 0) - middle).astype(F32).astype(BF16)
    wanted = jnp.broadcast_to(slot - middle, (tiles * TILE, own)).astype(BF16)
    hot = jnp.where(line == wanted, jnp.asarray(1, BF16), jnp.asarray(0, BF16))
    placed = lax.dot_general(hot, values, NT, preferred_element_type=F32).astype(BF16)
    places = [where[block, t] for t in range(tiles)]
    for t in range(tiles):
        to = pl.multiple_of(places[t], TILE)
        out[pl.ds(to, TILE), :] = placed[t * TILE : (t + 1) * TILE]


def sort_bins_kernel(nr, nf, lo, sub, tiles, where, *refs):
    bins = refs[:nr]
    slots, out = refs[nr:]
    own_feats = (bins[0].shape[0] - nf) // nf
    copies = LANES // own_feats
    cuts = slots.shape[0] * lo // (nr * nf)
    feat = lax.axis_index("feat")
    for j in range(nr):

        def sort_pair(jz):
            pair = []
            for jx in range(lo):
                k = jnp.bitwise_xor(feat, jz * lo + jx)
                pair.append(bins[j][pl.ds(pl.multiple_of(k * own_feats, own_feats), own_feats), :])
            for c, values in enumerate(cut_pair(pair, sub)):
                part = (j * (nf // lo) + jz) * cuts + c
                values = jnp.concatenate([values] * copies, axis=0)
                put_block(values, slots[pl.ds(part, 1), :], tiles, where, part, out)

        each(nf // lo, 4, sort_pair)


def put_grads(sizes, jc, where, source, parents, slots, leaf, grads):
    _, nf, ny, lo, hi, own, _, classes, nodes, tiles, sub = sizes
    me_feat = lax.axis_index("feat")
    code_row = hi * classes
    rest = leaf[...]
    leaf_parts = []
    for _ in range(3):
        leaf_parts.append(rest.astype(BF16))
        rest = rest - leaf_parts[-1].astype(F32)
    leaf_parts = jnp.concatenate(leaf_parts, axis=1)
    grads[...] = jnp.zeros(grads.shape, BF16)

    def put_rows(jy):
        j = jy * 2 + jc
        pair, ready = [], []
        for jz, jx in [(jz, jx) for jz in range(hi) for jx in range(lo)]:
            yx = jy * lo + jx
            k = jnp.bitwise_xor(me_feat, jz * lo + jx)
            block = j * nf + k
            margins = source[yx, jz * classes : (jz + 1) * classes, :]
            code = source[jy * lo, pl.ds(code_row + k, 1), :]
            for other in range(1, lo):
                code = code + source[jy * lo + other, pl.ds(code_row + k, 1), :]
            label = jnp.floor(code * 0.5)
            right = code - 2.0 * label
            node = 2.0 * parents[pl.ds(block, 1), :] + right
            node_hot = (node == iota((nodes, own), 0).astype(F32)).astype(F32).astype(BF16)
            moved = jnp.dot(leaf_parts, jnp.concatenate([node_hot] * 3, axis=0), preferred_element_type=F32)
            logits = margins + moved
            powers = jnp.exp(logits - jnp.max(logits, axis=0, keepdims=True))
            prob = powers * (1.0 / jnp.sum(powers, axis=0, keepdims=True))
            hot = label == iota((classes, own), 0).astype(F32)
            gradient = prob - jnp.where(hot, 1.0, 0.0)
            hessian = 2.0 * prob * (1.0 - prob)
            member = node - GROUP_NODES * jnp.floor(node * (1.0 / GROUP_NODES))
            member = jnp.broadcast_to(member, (classes, own)).astype(BF16)
            none = jnp.zeros((classes, own), BF16)
            parts = []
            for value in (gradient.astype(BF16), hessian.astype(BF16)):
                parts += [jnp.where(member == jnp.asarray(n, BF16), value, none) for n in range(GROUP_NODES)]
            pair.append(jnp.concatenate(parts, axis=0))
            if jx < lo - 1:
                continue
            ready.append((jz, cut_pair(pair, sub)))
            pair = []
        for jz, cuts in ready:
            for c, columns in enumerate(cuts):
                part = (j * hi + jz) * len(cuts) + c
                put_block(columns, slots[pl.ds(part, 1), :], tiles, where, part, grads)

    each(ny, 2, put_rows)


def near_kernel(sizes, where, near, parents, slots, leaf, grads):
    put_grads(sizes, 0, where, near, parents, slots, leaf, grads)


def level_kernel(sizes, where, chunks, near_grads, far, parents, slots, bins, leaf, gains, totals, grads, acc):
    _, _, _, _, _, _, own_feats, classes, nodes, _, _ = sizes
    groups = nodes // GROUP_NODES
    half = GROUP_NODES * classes
    width = BINS * own_feats
    put_grads(sizes, 1, where, far, parents, slots, leaf, grads)
    bins_per = LANES // own_feats
    lane_bin = (iota((1, LANES), 1) // own_feats).astype(F32)
    one, none = jnp.asarray(1, BF16), jnp.asarray(0, BF16)
    member = (iota((8, half), 1) // classes == iota((8, half), 0)).astype(F32)
    member = jnp.concatenate([member] * 3, axis=1).astype(BF16)

    @pl.loop(0, groups)
    def _(q):
        first = chunks[0, q]

        @pl.when(chunks[1, q] == 0)
        def _():
            acc[q] = jnp.zeros(acc.shape[1:], F32)

        def add_rows(at, rows):
            at = pl.multiple_of(at * CHUNK, CHUNK)
            fresh = at == first * CHUNK
            columns = near_grads[pl.ds(at, rows), :] + grads[pl.ds(at, rows), :]
            value = (bins[pl.ds(at, rows), :].astype(F32) - lane_bin).astype(BF16).T
            for m in range(width // COLS):
                below = []
                for s in range(COLS // LANES):
                    limit = (m * (COLS // LANES) + s) * bins_per
                    below.append(jnp.where(value <= jnp.asarray(limit, BF16), one, none))
                below = jnp.concatenate(below, axis=0)
                span = slice(m * COLS, (m + 1) * COLS)
                so_far = jnp.where(fresh, 0.0, acc[q, span, :])
                acc[q, span, :] = so_far + jnp.dot(below, columns, preferred_element_type=F32)

        length = chunks[1, q]
        largest = PIECES[0] // CHUNK

        @pl.loop(0, length // largest)
        def _(i):
            add_rows(first + i * largest, PIECES[0])

        for rows in PIECES[1:]:
            units = rows // CHUNK

            @pl.when((length // units) % 2 == 1)
            def _():
                add_rows(first + length // (2 * units) * (2 * units), rows)

        whole = acc[q, width - 1 : width, :]
        totals[q] = whole
        grad_whole = whole[:, :half]
        hess_whole = whole[:, half:]
        parent_score = grad_whole * grad_whole / (hess_whole + hess_ridge)
        for m in range(width // LANES):
            span = slice(m * LANES, (m + 1) * LANES)
            grad_left = acc[q, span, :half]
            hess_left = acc[q, span, half:]
            grad_right = grad_whole - grad_left
            hess_right = hess_whole - hess_left
            rest = (
                grad_left * grad_left / (hess_left + hess_ridge)
                + grad_right * grad_right / (hess_right + hess_ridge)
                - parent_score
            )
            parts = []
            for _ in range(3):
                parts.append(rest.astype(BF16))
                rest = rest - parts[-1].astype(F32)
            parts = jnp.concatenate(parts, axis=1)
            total = lax.dot_general(member, parts, NT, preferred_element_type=F32)
            gains[q, :, span] = total[:GROUP_NODES] * (1.0 / classes)


def flip_by(value, index, count):
    step = 1
    while step < count:
        shaped = value.reshape((count // (2 * step), 2, step) + value.shape[1:])
        flipped = jnp.flip(shaped, axis=1)
        value = jnp.where((index // step) % 2 == 1, flipped, shaped).reshape(value.shape)
        step *= 2
    return value


def swap(value, axes, sizes, offsets):
    total = 1
    for size in sizes:
        total *= size
    flat = 0
    for size, offset in zip(sizes, offsets):
        flat = flat * size + offset
    return lax.ppermute(value, axes, [(i, i ^ flat) for i in range(total)])


def body(margins, labels, row_bins, parents, split_feature, split_bin, leaf_values):
    feat_dev, group_rows = row_bins.shape
    own, classes = margins.shape
    nodes = leaf_values.shape[0]
    parent_count = split_feature.shape[0]
    nf, nr = lax.axis_size("feat"), lax.axis_size("rows")
    row = lax.axis_index("rows")
    own_feats = feat_dev // nr
    lo, ny = 2, nr // 2
    hi = nf // lo
    groups = nodes // GROUP_NODES
    blocks = nr * nf
    width = BINS * own_feats
    axes, sizes = ("rows", "feat"), (nr, nf)

    message_rows = nf * own_feats + nf
    first_inputs = (split_feature, split_bin, margins.T, labels, row_bins, parents.reshape(1, group_rows))
    first, *sent = pl.pallas_call(
        functools.partial(first_kernel, nr, nf),
        out_shape=[jax.ShapeDtypeStruct((classes + nf, own), F32)]
        + [jax.ShapeDtypeStruct((message_rows, own), BF16)] * (nr - 1),
        in_specs=[pl.BlockSpec(memory_space=pltpu.HBM)] * 6,
        out_specs=[VMEM] * nr,
        scratch_shapes=[pltpu.SMEM(x.shape, x.dtype) for x in first_inputs[:2]]
        + [pltpu.VMEM(x.shape, x.dtype) for x in first_inputs[2:]]
        + [pltpu.SemaphoreType.DMA((6,))],
        compiler_params=pltpu.CompilerParams(vmem_limit_bytes=VMEM_WHOLE),
        name="first",
    )(*first_inputs)

    own_bins = pl.pallas_call(
        functools.partial(own_kernel, nf),
        out_shape=jax.ShapeDtypeStruct((message_rows, own), BF16),
        in_specs=[pl.BlockSpec(memory_space=pltpu.HBM), VMEM],
        out_specs=VMEM,
        scratch_shapes=[pltpu.VMEM((own_feats, group_rows), I32), pltpu.SemaphoreType.DMA],
        compiler_params=pltpu.CompilerParams(vmem_limit_bytes=VMEM_SMALL),
        name="own_bins",
    )(row_bins, parents.reshape(1, group_rows))
    bins_by = [own_bins]
    for j in range(1, nr):
        bins_by.append(swap(sent[j - 1], axes, sizes, (j, 0)))
    along_z = [first] + [swap(first, axes, sizes, (0, lo * j)) for j in range(1, hi)]

    all_parents = jnp.concatenate([b[nf * own_feats :] for b in bins_by]).astype(F32)

    second = jnp.concatenate([m[:classes] for m in along_z] + [sum(m[classes:] for m in along_z)], axis=0)
    plane = []
    for jy in range(ny):
        for jx in range(lo):
            plane.append(second if jy + jx == 0 else swap(second, axes, sizes, (2 * jy, jx)))
    near = jnp.stack(plane)
    far = swap(near, axes, sizes, (1, 0))

    sub = SUB if lo * own % SUB == 0 else own
    parts = blocks * own // sub
    tiles = sub // TILE + groups * (TILE - 1) // TILE
    spare = parts * tiles + groups * (CHUNK // TILE - 1)
    ordered_rows = (spare + 1) * TILE
    slots, where, chunks = pl.pallas_call(
        functools.partial(plan_kernel, groups, parent_count // groups, spare, nr, nf, lo, sub),
        out_shape=(
            jax.ShapeDtypeStruct((parts, sub), F32),
            jax.ShapeDtypeStruct((parts, LANES), I32),
            jax.ShapeDtypeStruct((8, LANES), I32),
        ),
        in_specs=[VMEM],
        out_specs=(VMEM,) * 3,
        compiler_params=pltpu.CompilerParams(vmem_limit_bytes=VMEM_SMALL),
        name="plan",
    )(all_parents)

    ordered_bins = pl.pallas_call(
        functools.partial(sort_bins_kernel, nr, nf, lo, sub, tiles),
        out_shape=jax.ShapeDtypeStruct((ordered_rows, LANES), BF16),
        in_specs=[SMEM] + [VMEM] * (nr + 1),
        out_specs=VMEM,
        compiler_params=pltpu.CompilerParams(vmem_limit_bytes=VMEM_SMALL),
        name="sort_bins",
    )(where, *bins_by, slots)

    columns = 2 * GROUP_NODES * classes
    level_bytes = ordered_rows * 2 * (2 * columns + LANES) + groups * width * columns * 4 + VMEM_MORE
    near_bytes = ordered_rows * 2 * columns + VMEM_MORE
    shape = (nr, nf, ny, lo, hi, own, own_feats, classes, nodes, tiles, sub)
    leaf_t = leaf_values.T
    near_grads = pl.pallas_call(
        functools.partial(near_kernel, shape),
        out_shape=jax.ShapeDtypeStruct((ordered_rows, columns), BF16),
        in_specs=[SMEM] + [VMEM] * 4,
        out_specs=VMEM,
        compiler_params=pltpu.CompilerParams(vmem_limit_bytes=near_bytes),
        name="near",
    )(where, near, all_parents, slots, leaf_t)

    gains, totals = pl.pallas_call(
        functools.partial(level_kernel, shape),
        out_shape=(
            jax.ShapeDtypeStruct((groups, GROUP_NODES, width), F32),
            jax.ShapeDtypeStruct((groups, 1, columns), F32),
        ),
        in_specs=[SMEM] * 2 + [VMEM] * 6,
        out_specs=(VMEM, VMEM),
        scratch_shapes=[
            pltpu.VMEM((ordered_rows, columns), BF16),
            pltpu.VMEM((groups, width, columns), F32),
        ],
        compiler_params=pltpu.CompilerParams(vmem_limit_bytes=level_bytes),
        name="level",
    )(where, chunks, near_grads, far, all_parents, slots, ordered_bins, leaf_t)

    node_totals = totals.reshape(groups, 2, GROUP_NODES, classes).transpose(0, 2, 1, 3).reshape(nodes, 2 * classes)

    kept_nodes = nodes // nr
    relative = flip_by(gains.reshape(nr, kept_nodes, width), row, nr)
    kept = [relative[0]] + [swap(relative[j], axes, sizes, (j, 0)) for j in range(1, nr)]
    kept = flip_by(jnp.stack(kept), row, nr).reshape(nr, kept_nodes, BINS, own_feats)
    split_gains = kept.transpose(1, 0, 3, 2).reshape(kept_nodes, feat_dev, BINS)
    return split_gains, node_totals


def solution(mesh):
    return jax.shard_map(
        body,
        mesh=mesh,
        in_specs=(
            P(("rows", "feat"), None),
            P(("rows", "feat")),
            P("feat", "rows"),
            P("rows"),
            P(),
            P(),
            P(),
        ),
        out_specs=(P("rows", "feat", None), P()),
        check_vma=False,
    )
```
